128 devices in a mesh: row: 8 (over y_lo, x), col: 16 (over y_hi, z, core).
Axes of the slice: x: 4, y: 4 (y_hi: 2, y_lo: 2; y = y_hi * 2 + y_lo), z: 4, core: 2. Of those that a mesh axis runs over, the one named last changes fastest.
Arguments:
- density_block_entries: bfloat16 [64, 32, 128, 128], P('row', 'col'), as said below
- density_cols: int32 [64, 32], P('row', 'col'), may hold values from 0 to 63, as said below
- hamilton_values: bfloat16 [64, 32, 128, 128], P('row', 'col'), as said below
- hamilton_cols: int32 [64, 32], P('row', 'col'), may hold values from 0 to 63, as said below
- filter_cols: int32 [64, 64], P('row', 'col'), may hold values from 0 to 63, as said below
Outputs:
- squared_density: bfloat16 [64, 64, 128, 128], P('row', 'col')
- mixed_product: bfloat16 [64, 64, 128, 128], P('row', 'col')
- gradient: bfloat16 [64, 32, 128, 128], P('row', 'col')
The draws below stay inside these ranges and needn't reach their ends.
Inputs may be any that keep to these rules, and one draw needn't show every extreme that they name: `density_cols`: in every block row, slots c * 2 to (c + 1) * 2 - 1 hold distinct block columns of c * 4 to (c + 1) * 4 - 1. The pattern is symmetric: j is listed in row i exactly when i is listed in row j. `hamilton_cols`: in every block row, slots c * 2 to (c + 1) * 2 - 1 hold distinct block columns of c * 4 to (c + 1) * 4 - 1. The pattern is symmetric: j is listed in row i exactly when i is listed in row j. `filter_cols`: in every block row, slots c * 4 to (c + 1) * 4 - 1 hold distinct block columns of c * 4 to (c + 1) * 4 - 1. `density_block_entries`: the density matrix is symmetric: the block of row i and column j is the transpose of the block of row j and column i. `hamilton_values`: the Hamiltonian is symmetric: the block of row i and column j is the transpose of the block of row j and column i.
All inputs are finite; a program needn't handle non-finite values.
Results may differ from the reference program's by a relative error of at most 0.015.
Values may be sent and summed in bfloat16 or wider, within the bound.
A program may use at most 128 MiB of HBM per device.

```python
import jax
import jax.numpy as jnp
from jax import lax

BS = 128
BC = 4
KA = 2
KH = 2
KF = 4
NB = 64


def block_pattern(key, tag, count):
    folded = jax.random.fold_in(key, tag)
    offset_key, shift_key = jax.random.split(folded)
    offsets = jax.random.permutation(offset_key, BC)[:count].astype(jnp.int32)
    group_count = NB // BC
    drawn = jax.random.randint(shift_key, (group_count, group_count), 0, BC)
    shifts = jnp.triu(drawn) + jnp.triu(drawn, 1).T
    row_numbers = jnp.arange(NB, dtype=jnp.int32)
    group_starts = jnp.arange(group_count, dtype=jnp.int32) * BC
    row_shifts = shifts[row_numbers // BC]
    slot_location = (offsets[None, None, :] - row_numbers[:, None, None] - group_starts[None, :, None] - row_shifts[:, :, None]) % BC
    return (group_starts[None, :, None] + slot_location).reshape(NB, group_count * count).astype(jnp.int32)


def block_values(key, tag, columns, scale):
    row_numbers = jnp.arange(NB, dtype=jnp.int32)[:, None] + jnp.zeros_like(columns)
    lower = jnp.minimum(row_numbers, columns)
    higher = jnp.maximum(row_numbers, columns)
    pairing = (lower * NB + higher).reshape(-1)
    folded = jax.random.fold_in(key, tag)

    def single_block(pair_index):
        pair_key = jax.random.fold_in(folded, pair_index)
        return jax.random.normal(pair_key, (BS, BS), jnp.float32)
    blocks = jax.vmap(single_block)(pairing).reshape(NB, columns.shape[1], BS, BS)
    turned = jnp.swapaxes(blocks, 2, 3)
    above = (row_numbers > columns)[:, :, None, None]
    diagonal = (row_numbers == columns)[:, :, None, None]
    is_symmetric_matrix = jnp.where(diagonal, (blocks + turned) * 0.7071, jnp.where(above, turned, blocks))
    return (is_symmetric_matrix * scale).astype(jnp.bfloat16)


def draw_density_cols(key, part):
    return block_pattern(key, 1, KA)


def draw_hamilton_cols(key, part):
    return block_pattern(key, 2, KH)


def draw_filter_cols(key, part):
    return block_pattern(key, 3, KF)


def draw_density_block_entries(key, part):
    scale = (BS * (NB // BC) * KA * KA / BC) ** (-0.25)
    return block_values(key, 11, block_pattern(key, 1, KA), scale)


def draw_hamilton_values(key, part):
    scale = (BS * (NB // BC) * KF * KH / BC) ** (-0.5)
    return block_values(key, 12, block_pattern(key, 2, KH), scale)


def setup_inputs(seed: int = 0) -> dict:
    seeds = jax.random.split(jax.random.key(seed), 6)
    density_block_entries = draw_density_block_entries(jax.random.fold_in(seeds[5], 71), 0)
    density_cols = draw_density_cols(jax.random.fold_in(seeds[5], 71), 0)
    hamilton_values = draw_hamilton_values(jax.random.fold_in(seeds[5], 71), 0)
    hamilton_cols = draw_hamilton_cols(jax.random.fold_in(seeds[5], 71), 0)
    filter_cols = draw_filter_cols(jax.random.fold_in(seeds[5], 71), 0)
    return dict(density_block_entries=density_block_entries, density_cols=density_cols, hamilton_values=hamilton_values, hamilton_cols=hamilton_cols, filter_cols=filter_cols)


def block_products(left_vals, left_cols, right_vals, right_cols):
    chosen = right_vals[left_cols].astype(jnp.float32)
    block_product_list = jnp.einsum("sab,stbc->stac", left_vals.astype(jnp.float32), chosen, precision=lax.Precision.HIGHEST)
    return block_product_list.reshape(-1, BS, BS), right_cols[left_cols].reshape(-1)


def to_slots(block_product_list, product_cols, targets):
    filter_picker = (targets[:, None] == product_cols[None, :]).astype(jnp.float32)
    return jnp.einsum("wv,vug->wug", filter_picker, block_product_list, precision=lax.Precision.HIGHEST)


def reference(density_block_entries, density_cols, hamilton_values, hamilton_cols, filter_cols):
    def first_pass(row_index):
        left_vals = density_block_entries[row_index]
        left_cols = density_cols[row_index]
        square_terms, square_cols = block_products(left_vals, left_cols, density_block_entries, density_cols)
        mixed_terms, mixed_cols = block_products(left_vals, left_cols, hamilton_values, hamilton_cols)
        square_slots = to_slots(square_terms, square_cols, filter_cols[row_index]).astype(jnp.bfloat16)
        mixed_slots = to_slots(mixed_terms, mixed_cols, filter_cols[row_index]).astype(jnp.bfloat16)
        direct_slots = to_slots(mixed_terms, mixed_cols, left_cols)
        return square_slots, mixed_slots, direct_slots

    row_numbers = jnp.arange(NB, dtype=jnp.int32)
    square_term, mixed_term, direct_term = lax.map(first_pass, row_numbers)

    def second_pass(row_index):
        cubic_terms, cubic_cols = block_products(square_term[row_index], filter_cols[row_index], hamilton_values, hamilton_cols)
        return to_slots(cubic_terms, cubic_cols, density_cols[row_index])

    cubic_term = lax.map(second_pass, row_numbers)
    gradient = (3.0 * direct_term - 2.0 * cubic_term).astype(jnp.bfloat16)
    return square_term, mixed_term, gradient
```

```python
import jax
import jax.numpy as jnp
from jax import lax
from jax.experimental import pallas as pl
from jax.experimental.pallas import tpu as pltpu
from jax.sharding import PartitionSpec as P

MESH = pl.DeviceIdType.MESH
BF16, F32 = jnp.bfloat16, jnp.float32
BS = 128
RB, CB = 8, 4
NR, NC = 8, 16
KS = 2
HALF = 4 * KS * BS
IND = 4 * KS * CB
SH = HALF + IND
ROWS, COLS, CHUNK = RB * BS, CB * BS, RB * BS


def remote(src, dst, send, recv, dev):
    return pltpu.make_async_remote_copy(
        src_ref=src, dst_ref=dst, send_sem=send, recv_sem=recv,
        device_id=dev, device_id_type=MESH,
    )


def kernel(dv, di, hv, hi, filt, dcols, s_out, m_out, g_out,
           Dcol, Hcol, Drow, Srow, relay, Ld, Rd, Hd, accS, accM, accC,
           loc, xs, xr, zs, zr, hs, hr, ts, tr, cs, cr, es, er, us, ur, vs, vr):
    row, col = lax.axis_index("row"), lax.axis_index("col")
    x, ylo = row % 4, row // 4
    core, z, yhi = col % 2, (col // 2) % 4, col // 8

    def ridx(f, d):
        yy = (1 - ylo) if f else ylo
        return yy * 4 + (x + d + 4) % 4

    def cidx(f, d, other=False):
        yy = (1 - yhi) if f else yhi
        cc = (1 - core) if other else core
        return yy * 8 + ((z + d + 4) % 4) * 2 + cc

    xp, xm = (ridx(0, 1), col), (ridx(0, -1), col)
    zp, zm = (row, cidx(0, 1)), (row, cidx(0, -1))
    ylod = (ridx(1, 0), col)
    yind = (ridx(1, 0), cidx(1, 0))
    twin = (row, cidx(0, 0, True))

    local = [
        pltpu.make_async_copy(dv, Dcol.at[row, :, pl.ds(0, HALF), :], loc.at[0]),
        pltpu.make_async_copy(di, Dcol.at[row, :, pl.ds(HALF, IND), :], loc.at[1]),
        pltpu.make_async_copy(dv, Drow.at[col, :, pl.ds(0, HALF), :], loc.at[2]),
        pltpu.make_async_copy(di, Drow.at[col, :, pl.ds(HALF, IND), :], loc.at[3]),
        pltpu.make_async_copy(hv, Hcol.at[row, :, pl.ds(0, HALF), :], loc.at[4]),
        pltpu.make_async_copy(hi, Hcol.at[row, :, pl.ds(HALF, IND), :], loc.at[5]),
    ]
    for c in local:
        c.start()
    barrier = pltpu.get_barrier_semaphore()
    for dev in (xp, xm, zp, zm, ylod, yind, twin):
        pl.semaphore_signal(barrier, inc=1, device_id=dev, device_id_type=MESH)
    accS[...] = jnp.zeros_like(accS)
    accM[...] = jnp.zeros_like(accM)
    accC[...] = jnp.zeros_like(accC)
    for c in local:
        c.wait()
    pl.semaphore_wait(barrier, 7)

    sends = []

    def push(ref, idx, half, send, recv, dev):
        view = ref.at[idx] if half is None else ref.at[idx, half]
        c = remote(view, view, send, recv, dev)
        c.start()
        sends.append(c)

    def got(ref, idx, half, recv):
        view = ref.at[idx] if half is None else ref.at[idx, half]
        remote(view, view, recv, recv, twin).wait_recv()

    X = lambda i: (xs.at[i], xr.at[i])
    Z = lambda i: (zs.at[i], zr.at[i])
    H = lambda i: (hs.at[i], hr.at[i])
    T = lambda i: (ts.at[i], tr.at[i])
    C = lambda i: (cs.at[i], cr.at[i])
    E = lambda i: (es.at[i], er.at[i])
    U = lambda i: (us.at[i], ur.at[i])
    V = lambda i: (vs.at[i], vr.at[i])

    def tslot(f, d):
        return (4 if f else 0) + (d + 4) % 4

    def twin_push(ref, S, f, d):
        push(ref, cidx(f, d), None, *S(tslot(f, d)), twin)

    def twin_got(ref, R, f, d):
        got(ref, cidx(f, d, True), None, R.at[tslot(f, d)])

    push(Dcol, row, 0, *X(0), ylod)
    push(Dcol, row, 1, *X(1), ylod)
    push(Dcol, row, None, *X(2), xp)
    push(Dcol, row, None, *X(3), xm)
    push(Drow, col, None, *Z(2), zp)
    push(Drow, col, None, *Z(3), zm)
    twin_push(Drow, C, 0, 0)

    P_ = ridx(1, 0)
    for h in (0, 1):
        got(Dcol, P_, h, xr.at[h])
        c = remote(Dcol.at[P_, h], Drow.at[col, h], zs.at[h], zr.at[h], yind)
        c.start()
        sends.append(c)
    push(Dcol, P_, None, *X(4), xp)
    push(Dcol, P_, None, *X(5), xm)
    got(Dcol, ridx(0, -1), None, xr.at[2])
    push(Dcol, ridx(0, -1), 0, *X(6), xp)
    got(Dcol, ridx(0, 1), None, xr.at[3])
    push(Dcol, ridx(0, 1), 1, *X(7), xm)
    got(Drow, cidx(0, -1), None, zr.at[2])
    push(Drow, cidx(0, -1), 0, *Z(6), zp)
    twin_push(Drow, C, 0, -1)
    got(Drow, cidx(0, 1), None, zr.at[3])
    push(Drow, cidx(0, 1), 1, *Z(7), zm)
    twin_push(Drow, C, 0, 1)
    Q_ = cidx(1, 0)
    got(Drow, Q_, 0, zr.at[0])
    push(Drow, Q_, 0, *Z(10), zp)
    push(Drow, Q_, 0, *Z(11), zm)
    got(Drow, Q_, 1, zr.at[1])
    push(Drow, Q_, 1, *Z(12), zp)
    push(Drow, Q_, 1, *Z(13), zm)
    twin_push(Drow, C, 1, 0)
    got(Dcol, ridx(1, -1), None, xr.at[4])
    push(Dcol, ridx(1, -1), 0, *X(8), xp)
    got(Dcol, ridx(1, 1), None, xr.at[5])
    push(Dcol, ridx(1, 1), 1, *X(9), xm)
    push(Hcol, row, None, *H(0), ylod)
    push(Hcol, row, None, *H(2), xp)
    push(Hcol, row, None, *H(3), xm)
    got(Drow, cidx(1, -1), 0, zr.at[10])
    got(Drow, cidx(1, -1), 1, zr.at[12])
    push(Drow, cidx(1, -1), 0, *Z(8), zp)
    twin_push(Drow, C, 1, -1)
    got(Drow, cidx(1, 1), 0, zr.at[11])
    got(Drow, cidx(1, 1), 1, zr.at[13])
    push(Drow, cidx(1, 1), 1, *Z(9), zm)
    twin_push(Drow, C, 1, 1)
    for f in (0, 1):
        for d in (0, -1, 1):
            twin_got(Drow, cr, f, d)

    def spread(src, idx, dst, lane):
        def body(half, carry):
            for ii in range(4):
                b0 = src[idx, half, pl.ds(ii * 256, BS), :]
                b1 = src[idx, half, pl.ds(ii * 256 + BS, BS), :]
                at = pl.ds(pl.multiple_of(half * 512 + ii * BS, BS), BS)
                ind = src[idx, half, pl.ds(HALF, IND), :].astype(F32)
                for t in range(CB):
                    k = ii * 8 + t
                    i0 = jnp.broadcast_to(ind[k:k + 1], (16, BS)).astype(BF16)
                    i1 = jnp.broadcast_to(ind[k + 4:k + 5], (16, BS)).astype(BF16)
                    out = b0.reshape(8, 16, BS) * i0[None] + b1.reshape(8, 16, BS) * i1[None]
                    dst[at, pl.ds(lane + t * BS, BS)] = out.reshape(BS, BS)
            return carry
        lax.fori_loop(0, 2, body, 0)

    def mm(acc, left, right):
        def body(t, carry):
            at = pl.ds(pl.multiple_of(t * 512, 512), 512)
            acc[at, :] += jnp.dot(left[at, :], right[...], preferred_element_type=F32)
            return carry
        lax.fori_loop(0, ROWS // 512, body, 0)

    def left_panel(k):
        spread(Drow, 2 * k, Ld, 0)
        spread(Drow, 2 * k + 1, Ld, COLS)

    dz = (z - x + 4) % 4
    o0 = (dz // 2) * (1 - dz % 2)
    o1 = 1 + 2 * (dz // 2)
    o2 = 4 - o0 - o1

    def order(n):
        b = n // 2
        e0 = (1 - b % 2) * (1 - b // 2)
        e1 = (b % 2) * (1 - b // 2)
        e2 = (1 - b % 2) * (b // 2)
        e3 = (b % 2) * (b // 2)
        return (n % 2) * 4 + (x + e0 * o0 + e1 * o1 + e2 * o2 + e3 * 2 + 4) % 4

    def s_chunk(n, carry):
        k = order(n)
        left_panel(k)
        spread(Dcol, k, Rd, 0)
        mm(accS, Ld, Rd)
        return carry

    lax.fori_loop(0, 4, s_chunk, 0)
    got(Drow, cidx(0, 2), 0, zr.at[6])
    got(Drow, cidx(0, 2), 1, zr.at[7])
    twin_push(Drow, C, 0, 2)
    got(Dcol, ridx(0, 2), 0, xr.at[6])
    got(Dcol, ridx(0, 2), 1, xr.at[7])
    got(Dcol, ridx(1, 2), 0, xr.at[8])
    got(Dcol, ridx(1, 2), 1, xr.at[9])
    got(Drow, cidx(1, 2), 0, zr.at[8])
    got(Drow, cidx(1, 2), 1, zr.at[9])
    twin_push(Drow, C, 1, 2)
    twin_got(Drow, cr, 0, 2)
    twin_got(Drow, cr, 1, 2)
    lax.fori_loop(4, 8, s_chunk, 0)

    Srow[col] = accS[...].astype(BF16).reshape(2, ROWS // 2, COLS)
    push(Srow, col, None, *U(2), zp)
    push(Srow, col, None, *U(3), zm)
    c0 = remote(Srow.at[col, 0], relay.at[0], es.at[0], er.at[0], ylod)
    c1 = remote(Srow.at[col, 1], relay.at[1], es.at[1], er.at[1], yind)
    for c in (c0, c1):
        c.start()
        sends.append(c)
    twin_push(Srow, V, 0, 0)

    got(Hcol, P_, None, hr.at[0])
    push(Hcol, P_, None, *H(4), xp)
    push(Hcol, P_, None, *H(5), xm)
    got(Hcol, ridx(0, -1), None, hr.at[2])
    push(Hcol, ridx(0, -1), 0, *H(6), xp)
    got(Hcol, ridx(0, 1), None, hr.at[3])
    push(Hcol, ridx(0, 1), 1, *H(7), xm)

    def m_chunk(k):
        left_panel(k)
        spread(Hcol, k, Hd.at[k], 0)
        mm(accM, Ld, Hd.at[k])

    def m_near(n, carry):
        m_chunk((n % 2) * 4 + (x + n // 2 + (n // 2) // 2) % 4)
        return carry

    def m_near_own(n, carry):
        b = n // 2
        m_chunk(((ylo + n) % 2) * 4 + (x + b + b // 2) % 4)
        return carry

    m_chunk(row)
    got(relay, 0, None, er.at[0])
    c = remote(relay.at[0], Srow.at[col, 0], us.at[0], ur.at[0], yind)
    c.start()
    sends.append(c)
    got(relay, 1, None, er.at[1])
    c = remote(relay.at[1], Srow.at[Q_, 1], us.at[1], ur.at[1], ylod)
    c.start()
    sends.append(c)
    m_chunk(P_)
    got(Hcol, ridx(1, -1), None, hr.at[4])
    push(Hcol, ridx(1, -1), 0, *H(8), xp)
    got(Hcol, ridx(1, 1), None, hr.at[5])
    push(Hcol, ridx(1, 1), 1, *H(9), xm)
    got(Srow, cidx(0, -1), None, ur.at[2])
    push(Srow, cidx(0, -1), 0, *U(6), zp)
    twin_push(Srow, V, 0, -1)
    got(Srow, cidx(0, 1), None, ur.at[3])
    push(Srow, cidx(0, 1), 1, *U(7), zm)
    twin_push(Srow, V, 0, 1)
    got(Srow, Q_, 0, ur.at[0])
    got(Srow, Q_, 1, ur.at[1])
    push(Srow, Q_, None, *U(4), zp)
    push(Srow, Q_, None, *U(5), zm)
    twin_push(Srow, V, 1, 0)

    def m_mid(n, carry):
        m_chunk((n % 2) * 4 + (x + 1 + 2 * (n // 2)) % 4)
        return carry

    lax.fori_loop(0, 4, m_mid, 0)
    got(Hcol, ridx(0, 2), 0, hr.at[6])
    got(Hcol, ridx(0, 2), 1, hr.at[7])
    got(Hcol, ridx(1, 2), 0, hr.at[8])
    got(Hcol, ridx(1, 2), 1, hr.at[9])

    def m_far(n, carry):
        m_chunk(n * 4 + (x + 2) % 4)
        return carry

    lax.fori_loop(0, 2, m_far, 0)

    def pick(acc, i, which):
        at = pl.ds(pl.multiple_of(i * BS, BS), BS)
        place = jnp.broadcast_to(which, (BS, BS))
        out = acc[at, pl.ds(0, BS)]
        for t in range(1, CB):
            out = jnp.where(place == t, acc[at, pl.ds(t * BS, BS)], out)
        return out

    def filtered(i, carry):
        for w in range(CB):
            which = filt[i, w:w + 1, :]
            s_out[i * CB + w] = pick(accS, i, which).astype(BF16)
            m_out[i * CB + w] = pick(accM, i, which).astype(BF16)
        return carry

    lax.fori_loop(0, RB, filtered, 0)

    def c_chunk(f, d):
        for c in (0, 1):
            k = cidx(f, d) - core + c
            def body(t, carry, k=k, c=c):
                at = pl.ds(pl.multiple_of(t * 512, 512), 512)
                accC[at, :] += jnp.dot(
                    Srow[k, t], Hd[k // 2, pl.ds(c * COLS, COLS), :],
                    preferred_element_type=F32)
                return carry
            lax.fori_loop(0, 2, body, 0)

    twin_got(Srow, vr, 0, 0)
    c_chunk(0, 0)
    twin_got(Srow, vr, 0, -1)
    c_chunk(0, -1)
    twin_got(Srow, vr, 0, 1)
    c_chunk(0, 1)
    twin_got(Srow, vr, 1, 0)
    c_chunk(1, 0)
    got(Srow, cidx(0, 2), 0, ur.at[6])
    got(Srow, cidx(0, 2), 1, ur.at[7])
    twin_push(Srow, V, 0, 2)
    got(Srow, cidx(1, -1), None, ur.at[4])
    push(Srow, cidx(1, -1), 0, *U(8), zp)
    twin_push(Srow, V, 1, -1)
    got(Srow, cidx(1, 1), None, ur.at[5])
    push(Srow, cidx(1, 1), 1, *U(9), zm)
    twin_push(Srow, V, 1, 1)
    twin_got(Srow, vr, 0, 2)
    c_chunk(0, 2)
    twin_got(Srow, vr, 1, -1)
    c_chunk(1, -1)
    twin_got(Srow, vr, 1, 1)
    c_chunk(1, 1)
    got(Srow, cidx(1, 2), 0, ur.at[8])
    got(Srow, cidx(1, 2), 1, ur.at[9])
    twin_push(Srow, V, 1, 2)
    twin_got(Srow, vr, 1, 2)
    c_chunk(1, 2)

    def gradient(i, carry):
        for s in range(KS):
            which = dcols[i, s:s + 1, :]
            g_out[i * KS + s] = (3.0 * pick(accM, i, which) - 2.0 * pick(accC, i, which)).astype(BF16)
        return carry

    lax.fori_loop(0, RB, gradient, 0)
    for c in sends:
        c.wait_send()


def local(density, density_cols, hamilton, hamilton_cols, filter_cols):
    base = lax.axis_index("col") * CB

    def indicators(cols):
        hit = cols[:, :, None] == base + jnp.arange(CB, dtype=jnp.int32)
        hit = jnp.broadcast_to(hit[..., None], (RB, KS, CB, BS))
        return hit.astype(BF16).reshape(2, IND, BS)

    def places(cols):
        return jnp.broadcast_to((cols - base)[:, :, None], cols.shape + (BS,))

    def values(v):
        return v.reshape(2, HALF, BS)

    hbm = pl.BlockSpec(memory_space=pl.ANY)
    vmem = pl.BlockSpec(memory_space=pltpu.VMEM)
    dma = lambda n: pltpu.SemaphoreType.DMA((n,))
    s, m, g = pl.pallas_call(
        kernel,
        out_shape=(
            jax.ShapeDtypeStruct((RB * CB, BS, BS), BF16),
            jax.ShapeDtypeStruct((RB * CB, BS, BS), BF16),
            jax.ShapeDtypeStruct((RB * KS, BS, BS), BF16),
        ),
        in_specs=[hbm] * 4 + [vmem] * 2,
        out_specs=(vmem,) * 3,
        scratch_shapes=[
            pltpu.VMEM((NR, 2, SH, BS), BF16),
            pltpu.VMEM((NR, 2, SH, BS), BF16),
            pltpu.VMEM((NC, 2, SH, BS), BF16),
            pltpu.VMEM((NC, 2, ROWS // 2, COLS), BF16),
            pltpu.VMEM((2, ROWS // 2, COLS), BF16),
            pltpu.VMEM((ROWS, CHUNK), BF16),
            pltpu.VMEM((CHUNK, COLS), BF16),
            pltpu.VMEM((NR, CHUNK, COLS), BF16),
            pltpu.VMEM((ROWS, COLS), F32),
            pltpu.VMEM((ROWS, COLS), F32),
            pltpu.VMEM((ROWS, COLS), F32),
            dma(6),
            dma(10), dma(10), dma(14), dma(14), dma(10), dma(10), dma(1), dma(1),
            dma(8), dma(8), dma(2), dma(2), dma(10), dma(10), dma(8), dma(8),
        ],
        compiler_params=pltpu.CompilerParams(
            collective_id=0, has_side_effects=True, vmem_limit_bytes=66_000_000),
    )(values(density), indicators(density_cols), values(hamilton),
      indicators(hamilton_cols), places(filter_cols), places(density_cols))
    return (s.reshape(RB, CB, BS, BS), m.reshape(RB, CB, BS, BS), g.reshape(RB, KS, BS, BS))


def solution(mesh):
    blocks, cols = P("row", "col", None, None), P("row", "col")
    return jax.shard_map(
        local, mesh=mesh, in_specs=(blocks, cols, blocks, cols, cols),
        out_specs=(blocks,) * 3, check_vma=False)
```

```python
import jax
import jax.numpy as jnp
from jax import lax
from jax.experimental import pallas as pl
from jax.experimental.pallas import tpu as pltpu
from jax.sharding import PartitionSpec as P

MESH = pl.DeviceIdType.MESH
BF16, F32 = jnp.bfloat16, jnp.float32
BS = 128
RB, CB = 8, 4
NR, NC = 8, 16
KS = 2
HALF = 4 * KS * BS
IND = 4 * KS * CB
SH = HALF + IND
NP = 8
JP = BS // NP
ROWS, COLS, CHUNK = RB * BS, CB * BS, RB * BS


def remote(src, dst, send, recv, dev):
    return pltpu.make_async_remote_copy(
        src_ref=src, dst_ref=dst, send_sem=send, recv_sem=recv,
        device_id=dev, device_id_type=MESH,
    )


def kernel(dv, di, hv, hi, filt, dcols, s_out, m_out, g_out,
           Dcol, Hcol, Drow, Htw, Hti, Sown, Stw, Dd, Rd, Hr0, Hr1, accS, accM, CT,
           PB, Al, Ar, Bl, Br, Y, cub,
           loc, xs, xr, zs, zr, hs, hr, cs, cr, ts, tr, as_, ar, bs, br, ys, yr):
    row, col = lax.axis_index("row"), lax.axis_index("col")
    x, ylo = row % 4, row // 4
    core, z, yhi = col % 2, (col // 2) % 4, col // 8

    def ridx(f, d):
        yy = (1 - ylo) if f else ylo
        return yy * 4 + (x + d + 4) % 4

    def cidx(f, d, other=False):
        yy = (1 - yhi) if f else yhi
        cc = (1 - core) if other else core
        return yy * 8 + ((z + d + 4) % 4) * 2 + cc

    xp, xm = (ridx(0, 1), col), (ridx(0, -1), col)
    zp, zm = (row, cidx(0, 1)), (row, cidx(0, -1))
    ylod = (ridx(1, 0), col)
    yind = (ridx(1, 0), cidx(1, 0))
    yhid = (row, cidx(1, 0))
    twin = (row, cidx(0, 0, True))

    first = [
        pltpu.make_async_copy(dv, Dcol.at[row, :, pl.ds(0, HALF), :], loc.at[0]),
        pltpu.make_async_copy(di, Dcol.at[row, :, pl.ds(HALF, IND), :], loc.at[1]),
        pltpu.make_async_copy(hi, Dcol.at[row, :, pl.ds(SH, IND), :], loc.at[2]),
        pltpu.make_async_copy(dv, Drow.at[col, :, pl.ds(0, HALF), :], loc.at[3]),
        pltpu.make_async_copy(di, Drow.at[col, :, pl.ds(HALF, IND), :], loc.at[4]),
    ]
    later = [
        pltpu.make_async_copy(hv.at[:, :, q], Hcol.at[q, row], loc.at[5 + q])
        for q in range(NP)
    ]
    for c in first + later:
        c.start()
    barrier = pltpu.get_barrier_semaphore()
    for dev in (xp, xm, zp, zm, ylod, yind, yhid, twin):
        pl.semaphore_signal(barrier, inc=1, device_id=dev, device_id_type=MESH)
    for c in first:
        c.wait()
    pl.semaphore_wait(barrier, 8)

    sends = []

    def push(view, send, recv, dev, there=None):
        c = remote(view, view if there is None else there, send, recv, dev)
        c.start()
        sends.append(c)

    def got(view, recv):
        remote(view, view, recv, recv, twin).wait_recv()

    def sent(view, send):
        remote(view, view, send, send, twin).wait_send()

    def dc(f, d, half=None):
        k = ridx(f, d)
        return Dcol.at[k] if half is None else Dcol.at[k, half]

    def dr(f, d, half=None, other=False):
        k = cidx(f, d, other)
        return Drow.at[k] if half is None else Drow.at[k, half]

    def X(view, i, dev):
        push(view, xs.at[i], xr.at[i], dev)

    def Z(view, i, dev):
        push(view, zs.at[i], zr.at[i], dev)

    def to_twin(f, d):
        i = f * 4 + (d + 4) % 4
        push(dr(f, d), cs.at[i], cr.at[i], twin)

    def from_twin(f, d):
        got(dr(f, d, other=True), cr.at[f * 4 + (d + 4) % 4])

    X(dc(0, 0, 0), 0, ylod)
    X(dc(0, 0, 1), 1, ylod)
    X(dc(0, 0), 2, xp)
    X(dc(0, 0), 3, xm)
    Z(dr(0, 0), 2, zp)
    Z(dr(0, 0), 3, zm)
    to_twin(0, 0)
    accS[...] = jnp.zeros_like(accS)
    accM[...] = jnp.zeros_like(accM)
    for c in later:
        c.wait()

    for h in (0, 1):
        got(dc(1, 0, h), xr.at[h])
        push(Dcol.at[ridx(1, 0), h, pl.ds(0, SH)], zs.at[h], zr.at[h], yind, Drow.at[col, h])
    X(dc(1, 0), 4, xp)
    X(dc(1, 0), 5, xm)
    got(dc(0, -1), xr.at[2])
    X(dc(0, -1, 0), 6, xp)
    got(dc(0, 1), xr.at[3])
    X(dc(0, 1, 1), 7, xm)
    got(dr(0, -1), zr.at[2])
    Z(dr(0, -1, 0), 6, zp)
    to_twin(0, -1)
    got(dr(0, 1), zr.at[3])
    Z(dr(0, 1, 1), 7, zm)
    to_twin(0, 1)
    for h in (0, 1):
        got(dr(1, 0, h), zr.at[h])
        Z(dr(1, 0, h), 10 + 2 * h, zp)
        Z(dr(1, 0, h), 11 + 2 * h, zm)
    to_twin(1, 0)
    got(dc(1, -1), xr.at[4])
    X(dc(1, -1, 0), 8, xp)
    got(dc(1, 1), xr.at[5])
    X(dc(1, 1, 1), 9, xm)

    def hp(q, f, d, half=None):
        k = ridx(f, d)
        return Hcol.at[q, k] if half is None else Hcol.at[q, k, half]

    H_OWN = ((0, 0, None, 0, ylod), (0, 0, None, 1, xp), (0, 0, None, 2, xm))
    H_MID = ((1, 0, None, 3, xp), (1, 0, None, 4, xm), (0, -1, 0, 5, xp), (0, 1, 1, 6, xm))
    H_FAR = ((1, -1, 0, 7, xp), (1, 1, 1, 8, xm))

    def h_push(q, f, d, half, i, dev):
        view = hp(q, f, d, half)
        remote(view, view, hs.at[q * 9 + i], hr.at[q * 9 + i], dev).start()

    def h_own(q):
        for a in H_OWN:
            h_push(q, *a)

    def h_mid(q):
        got(hp(q, 1, 0), hr.at[q * 9])
        h_push(q, *H_MID[0])
        h_push(q, *H_MID[1])
        got(hp(q, 0, -1), hr.at[q * 9 + 1])
        h_push(q, *H_MID[2])
        got(hp(q, 0, 1), hr.at[q * 9 + 2])
        h_push(q, *H_MID[3])

    def h_far(q):
        got(hp(q, 1, -1), hr.at[q * 9 + 3])
        h_push(q, *H_FAR[0])
        got(hp(q, 1, 1), hr.at[q * 9 + 4])
        h_push(q, *H_FAR[1])

    def h_end(q):
        got(hp(q, 0, 2, 0), hr.at[q * 9 + 5])
        got(hp(q, 0, 2, 1), hr.at[q * 9 + 6])
        got(hp(q, 1, 2, 0), hr.at[q * 9 + 7])
        got(hp(q, 1, 2, 1), hr.at[q * 9 + 8])

    for q in range(3):
        h_own(q)
    got(dr(1, -1, 0), zr.at[10])
    got(dr(1, -1, 1), zr.at[12])
    Z(dr(1, -1, 0), 8, zp)
    to_twin(1, -1)
    got(dr(1, 1, 0), zr.at[11])
    got(dr(1, 1, 1), zr.at[13])
    Z(dr(1, 1, 1), 9, zm)
    to_twin(1, 1)
    for f in (0, 1):
        for d in (0, -1, 1):
            from_twin(f, d)

    def spread(block, ind, store):
        for ii in range(4):
            b0, b1 = block(ii * 2), block(ii * 2 + 1)
            n = b0.shape[0] // 16
            for t in range(CB):
                k = ii * 8 + t
                i0 = jnp.broadcast_to(ind[k:k + 1], (16, BS)).astype(BF16)
                i1 = jnp.broadcast_to(ind[k + 4:k + 5], (16, BS)).astype(BF16)
                out = b0.reshape(n, 16, BS) * i0[None] + b1.reshape(n, 16, BS) * i1[None]
                store(ii, t, out.reshape(n * 16, BS))

    def spread_d(src, k, put):
        def body(half, carry):
            ind = src[k, half, pl.ds(HALF, IND), :].astype(F32)

            def store(ii, t, v):
                put(pl.ds(pl.multiple_of(half * 512 + ii * BS, BS), BS), t, v)

            spread(lambda b: src[k, half, pl.ds(b * BS, BS), :], ind, store)
            return carry
        lax.fori_loop(0, 2, body, 0)

    def put_r(at, t, v):
        Rd[at, pl.ds(t * BS, BS)] = v

    dz = (z - x + 4) % 4
    o0 = (dz // 2) * (1 - dz % 2)
    o1 = 1 + 2 * (dz // 2)
    o2 = 4 - o0 - o1

    def order(n):
        b = n // 2
        e0 = (1 - b % 2) * (1 - b // 2)
        e1 = (b % 2) * (1 - b // 2)
        e2 = (1 - b % 2) * (b // 2)
        e3 = (b % 2) * (b // 2)
        return (n % 2) * 4 + (x + e0 * o0 + e1 * o1 + e2 * o2 + e3 * 2 + 4) % 4

    def s_chunk(n, carry):
        k = order(n)
        for c in (0, 1):
            def put(at, t, v, c=c):
                Dd[k, at, pl.ds(c * COLS + t * BS, BS)] = v
            spread_d(Drow, 2 * k + c, put)
        spread_d(Dcol, k, put_r)
        accS[...] += jnp.dot(Dd[k], Rd[...], preferred_element_type=F32)

        @pl.when(n == 3)
        def _():
            got(dr(0, 2, 0), zr.at[6])
            got(dr(0, 2, 1), zr.at[7])
            remote(dr(0, 2), dr(0, 2), cs.at[2], cr.at[2], twin).start()
            for f in (0, 1):
                got(dc(f, 2, 0), xr.at[6 + 2 * f])
                got(dc(f, 2, 1), xr.at[7 + 2 * f])
            h_mid(0)
            h_mid(1)
            got(dr(1, 2, 0), zr.at[8])
            got(dr(1, 2, 1), zr.at[9])
            remote(dr(1, 2), dr(1, 2), cs.at[6], cr.at[6], twin).start()
            from_twin(0, 2)
            from_twin(1, 2)

        @pl.when(n == 5)
        def _():
            h_far(0)
            h_own(3)
            h_mid(2)

        return carry

    lax.fori_loop(0, 8, s_chunk, 0)

    Sown[...] = accS[...].astype(BF16)
    push(Sown, ts.at[NP], tr.at[NP], twin, Stw)
    push(Dcol.at[:, 1 - core, pl.ds(SH, IND)], ts.at[NP + 1], tr.at[NP + 1], twin, Hti)
    h_far(1)
    got(Stw, tr.at[NP])
    got(Hti, tr.at[NP + 1])

    def pick(acc, i, which):
        at = pl.ds(pl.multiple_of(i * BS, BS), BS)
        place = jnp.broadcast_to(which, (BS, BS))
        out = acc[at, pl.ds(0, BS)]
        for t in range(1, CB):
            out = jnp.where(place == t, acc[at, pl.ds(t * BS, BS)], out)
        return out

    def filtered(acc, out, i):
        for w in range(CB):
            out[i * CB + w] = pick(acc, i, filt[i, w:w + 1, :]).astype(BF16)

    NT = (((1,), (1,)), ((), ()))

    def partials(q):
        def rows(m, carry):
            def put(ref):
                def store(ii, t, v):
                    at = pl.ds(pl.multiple_of(m * 64 + ii * JP, JP), JP)
                    ref[at, pl.ds(t * BS, BS)] = v
                return store
            own = Dcol[m, core, pl.ds(SH, IND), :].astype(F32)
            spread(lambda b: Hcol[q, m, core, b], own, put(Hr0))
            spread(lambda b: Htw[q, m, b], Hti[m].astype(F32), put(Hr1))
            return carry
        lax.fori_loop(0, 8, rows, 0)
        CT[q % 3] = (
            lax.dot_general(Hr0[...], Sown[...], NT, preferred_element_type=F32)
            + lax.dot_general(Hr1[...], Stw[...], NT, preferred_element_type=F32)
        )

    def extract(q, m, half, emit):
        ind = Drow[2 * m + core, half, pl.ds(HALF, IND), :].astype(F32)
        for ii in range(4):
            lanes = pl.ds((half * 4 + ii) * BS, BS)
            v = [CT[q % 3, pl.ds(pl.multiple_of(m * 64 + t * JP, JP), JP), lanes] for t in range(CB)]
            for s in range(KS):
                out = v[0]
                for t in range(1, CB):
                    k = ii * 8 + s * 4 + t
                    hit = jnp.broadcast_to(ind[k:k + 1], (JP, BS)) > 0.5
                    out = jnp.where(hit, v[t], out)
                emit(ii * KS + s, out)

    def chip(f, d):
        hh = (1 - yhi) if f else yhi
        return hh * 4 + (z + d + 4) % 4

    def rs_far(q):
        for f in (1, 0):
            m = chip(f, 2)
            for half, (dev, dst) in enumerate(((zp, Al), (zm, Ar))):
                def emit(b, v, half=half):
                    PB[q, m, half * 8 + b] = v.astype(BF16)
                extract(q, m, half, emit)
                i = q * 4 + f * 2 + half
                remote(PB.at[q, m, pl.ds(half * 8, 8)], dst.at[q, f], as_.at[i], ar.at[i], dev).start()

    def rs_near(q):
        for f in (1, 0):
            for side, (d, dev, src, dst) in enumerate(((1, zp, Al, Bl), (-1, zm, Ar, Br))):
                m = chip(f, d)
                i = q * 4 + f * 2 + side
                got(src.at[q, f], ar.at[i])
                for half in (0, 1):
                    def emit(b, v, half=half):
                        if half == side:
                            v = v + src[q, f, b].astype(F32)
                        PB[q, m, half * 8 + b] = v.astype(BF16)
                    extract(q, m, half, emit)
                remote(PB.at[q, m], dst.at[q, f], bs.at[i], br.at[i], dev).start()

    def rs_own(q):
        for f in (1, 0):
            m = chip(f, 0)
            got(Bl.at[q, f], br.at[q * 4 + f * 2])
            got(Br.at[q, f], br.at[q * 4 + f * 2 + 1])
            for half in (0, 1):
                def emit(b, v, half=half):
                    b = half * 8 + b
                    v = v + Bl[q, f, b].astype(F32) + Br[q, f, b].astype(F32)
                    if f:
                        PB[q, m, b] = v.astype(BF16)
                    else:
                        cub[b, pl.ds(pl.multiple_of(q * JP, JP), JP), :] = v
                extract(q, m, half, emit)
            if f:
                remote(PB.at[q, m], Y.at[q], ys.at[q], yr.at[q], yhid).start()

    def m_chunk(k, carry):
        def body(half, c):
            ind = Dcol[k, half, pl.ds(SH, IND), :].astype(F32)

            def store(ii, t, v):
                Rd[pl.ds(pl.multiple_of(half * 512 + ii * BS, BS), BS), pl.ds(t * BS, BS)] = v

            spread(lambda b: Hcol[:, k, half, b].reshape(BS, BS), ind, store)
            return c
        lax.fori_loop(0, 2, body, 0)
        accM[...] += jnp.dot(Dd[k], Rd[...], preferred_element_type=F32)
        return carry

    def step(q, carry):
        @pl.when(q < NP)
        def _():
            h_end(q)
            remote(Hcol.at[q, :, 1 - core], Htw.at[q], ts.at[q], tr.at[q], twin).start()

        @pl.when(q + 2 < NP)
        def _():
            h_far(q + 2)

        @pl.when(q + 3 < NP)
        def _():
            h_mid(q + 3)

        @pl.when(q + 4 < NP)
        def _():
            h_own(q + 4)

        @pl.when(q < NP)
        def _():
            filtered(accS, s_out, q)
            got(Htw.at[q], tr.at[q])
            partials(q)
            rs_far(q)

        @pl.when((q >= 1) & (q < NP + 1))
        def _():
            rs_near(q - 1)

        @pl.when(q >= 2)
        def _():
            rs_own(q - 2)

        @pl.when(q >= NP - 1)
        def _():
            lo = (q - NP + 1) * 3
            lax.fori_loop(lo, lo + 3 - (q - NP + 1) // 2, m_chunk, 0)

        return carry

    lax.fori_loop(0, NP + 2, step, 0)

    def m_rows(i, carry):
        filtered(accM, m_out, i)
        return carry

    lax.fori_loop(0, RB, m_rows, 0)

    def y_wait(q, carry):
        got(Y.at[q], yr.at[q])
        return carry

    lax.fori_loop(0, NP, y_wait, 0)

    def gradient(i, carry):
        for s in range(KS):
            b = i * KS + s
            cubic = cub[b] + Y[:, b].reshape(BS, BS).astype(F32)
            direct = pick(accM, i, dcols[i, s:s + 1, :])
            g_out[b] = (3.0 * direct - 2.0 * cubic.T).astype(BF16)
        return carry

    lax.fori_loop(0, RB, gradient, 0)

    for c in sends:
        c.wait_send()

    def drain(q, carry):
        for f, d, half, i, dev in H_OWN + H_MID + H_FAR:
            sent(hp(q, f, d, half), hs.at[q * 9 + i])
        sent(Htw.at[q], ts.at[q])
        for i in range(4):
            sent(Al.at[q, 0], as_.at[q * 4 + i])
            sent(Bl.at[q, 0], bs.at[q * 4 + i])
        sent(Y.at[q], ys.at[q])
        return carry

    lax.fori_loop(0, NP, drain, 0)
    sent(dr(0, 2), cs.at[2])
    sent(dr(1, 2), cs.at[6])


def local(density, density_cols, hamilton, hamilton_cols, filter_cols):
    base = lax.axis_index("col") * CB

    def indicators(cols):
        hit = cols[:, :, None] == base + jnp.arange(CB, dtype=jnp.int32)
        hit = jnp.broadcast_to(hit[..., None], (RB, KS, CB, BS))
        return hit.astype(BF16).reshape(2, IND, BS)

    def places(cols):
        return jnp.broadcast_to((cols - base)[:, :, None], cols.shape + (BS,))

    def values(v):
        return v.reshape(2, HALF, BS)

    hbm = pl.BlockSpec(memory_space=pl.ANY)
    vmem = pl.BlockSpec(memory_space=pltpu.VMEM)
    dma = lambda n: pltpu.SemaphoreType.DMA((n,))
    s, m, g = pl.pallas_call(
        kernel,
        out_shape=(
            jax.ShapeDtypeStruct((RB * CB, BS, BS), BF16),
            jax.ShapeDtypeStruct((RB * CB, BS, BS), BF16),
            jax.ShapeDtypeStruct((RB * KS, BS, BS), BF16),
        ),
        in_specs=[hbm] * 4 + [vmem] * 2,
        out_specs=(vmem,) * 3,
        scratch_shapes=[
            pltpu.VMEM((NR, 2, SH + IND, BS), BF16),
            pltpu.VMEM((NP, NR, 2, 8, JP, BS), BF16),
            pltpu.VMEM((NC, 2, SH, BS), BF16),
            pltpu.VMEM((NP, NR, 8, JP, BS), BF16),
            pltpu.VMEM((NR, IND, BS), BF16),
            pltpu.VMEM((ROWS, COLS), BF16),
            pltpu.VMEM((ROWS, COLS), BF16),
            pltpu.VMEM((NR, ROWS, CHUNK), BF16),
            pltpu.VMEM((CHUNK, COLS), BF16),
            pltpu.VMEM((NR * CB * JP, COLS), BF16),
            pltpu.VMEM((NR * CB * JP, COLS), BF16),
            pltpu.VMEM((ROWS, COLS), F32),
            pltpu.VMEM((ROWS, COLS), F32),
            pltpu.VMEM((3, NR * CB * JP, ROWS), F32),
            pltpu.VMEM((NP, NR, RB * KS, JP, BS), BF16),
            pltpu.VMEM((NP, 2, RB, JP, BS), BF16),
            pltpu.VMEM((NP, 2, RB, JP, BS), BF16),
            pltpu.VMEM((NP, 2, RB * KS, JP, BS), BF16),
            pltpu.VMEM((NP, 2, RB * KS, JP, BS), BF16),
            pltpu.VMEM((NP, RB * KS, JP, BS), BF16),
            pltpu.VMEM((RB * KS, BS, BS), F32),
            dma(5 + NP), dma(10), dma(10), dma(14), dma(14), dma(9 * NP), dma(9 * NP),
            dma(8), dma(8), dma(NP + 2), dma(NP + 2), dma(4 * NP), dma(4 * NP),
            dma(4 * NP), dma(4 * NP), dma(NP), dma(NP),
        ],
        compiler_params=pltpu.CompilerParams(
            collective_id=0, has_side_effects=True, vmem_limit_bytes=67_000_000),
    )(values(density), indicators(density_cols),
      hamilton.reshape(2, 8, NP, JP, BS),
      indicators(hamilton_cols), places(filter_cols), places(density_cols))
    return (s.reshape(RB, CB, BS, BS), m.reshape(RB, CB, BS, BS), g.reshape(RB, KS, BS, BS))


def solution(mesh):
    blocks, cols = P("row", "col", None, None), P("row", "col")
    return jax.shard_map(
        local, mesh=mesh, in_specs=(blocks, cols, blocks, cols, cols),
        out_specs=(blocks,) * 3, check_vma=False)
```

```python
import jax
import jax.numpy as jnp
from jax import lax
from jax.experimental import pallas as pl
from jax.experimental.pallas import tpu as pltpu
from jax.sharding import PartitionSpec as P

MESH = pl.DeviceIdType.MESH
BF16, F32 = jnp.bfloat16, jnp.float32
BS = 128
RB, CB = 8, 4
NR, NC = 8, 16
KS = 2
HALF = 4 * KS * BS
IND = 4 * KS * CB
SH = HALF + IND
NP = 8
JP = BS // NP
ROWS, COLS, CHUNK = RB * BS, CB * BS, RB * BS


def remote(src, dst, send, recv, dev):
    return pltpu.make_async_remote_copy(
        src_ref=src, dst_ref=dst, send_sem=send, recv_sem=recv,
        device_id=dev, device_id_type=MESH,
    )


def kernel(dv, di, hv, hi, filt, dcols, s_out, m_out, g_out,
           Dcol, Hcol, Drow, Htw, Hti, Sown, Stw, Dd, Rd, Hr0, Hr1, accS, accM, CT,
           PB, OWN, Al, Ar, Bl, Br, Y, cub,
           loc, xs, xr, zs, zr, hs, hr, cs, cr, ts, tr, as_, ar, bs, br, ys, yr):
    row, col = lax.axis_index("row"), lax.axis_index("col")
    x, ylo = row % 4, row // 4
    core, z, yhi = col % 2, (col // 2) % 4, col // 8

    def ridx(f, d):
        yy = (1 - ylo) if f else ylo
        return yy * 4 + (x + d + 4) % 4

    def cidx(f, d, other=False):
        yy = (1 - yhi) if f else yhi
        cc = (1 - core) if other else core
        return yy * 8 + ((z + d + 4) % 4) * 2 + cc

    xp, xm = (ridx(0, 1), col), (ridx(0, -1), col)
    zp, zm = (row, cidx(0, 1)), (row, cidx(0, -1))
    ylod = (ridx(1, 0), col)
    yind = (ridx(1, 0), cidx(1, 0))
    yhid = (row, cidx(1, 0))
    twin = (row, cidx(0, 0, True))

    first = [
        pltpu.make_async_copy(dv, Dcol.at[row, :, pl.ds(0, HALF), :], loc.at[0]),
        pltpu.make_async_copy(di, Dcol.at[row, :, pl.ds(HALF, IND), :], loc.at[1]),
        pltpu.make_async_copy(hi, Dcol.at[row, :, pl.ds(SH, IND), :], loc.at[2]),
        pltpu.make_async_copy(dv, Drow.at[col, :, pl.ds(0, HALF), :], loc.at[3]),
        pltpu.make_async_copy(di, Drow.at[col, :, pl.ds(HALF, IND), :], loc.at[4]),
    ]
    later = [
        pltpu.make_async_copy(hv.at[:, :, q], Hcol.at[q, row], loc.at[5 + q])
        for q in range(NP)
    ]
    for c in first + later:
        c.start()
    barrier = pltpu.get_barrier_semaphore()
    for dev in (xp, xm, zp, zm, ylod, yind, yhid, twin):
        pl.semaphore_signal(barrier, inc=1, device_id=dev, device_id_type=MESH)
    for c in first:
        c.wait()
    pl.semaphore_wait(barrier, 8)

    sends = []

    def push(view, send, recv, dev, there=None):
        c = remote(view, view if there is None else there, send, recv, dev)
        c.start()
        sends.append(c)

    def got(view, recv):
        remote(view, view, recv, recv, twin).wait_recv()

    def sent(view, send):
        remote(view, view, send, send, twin).wait_send()

    def dc(f, d, half=None):
        k = ridx(f, d)
        return Dcol.at[k] if half is None else Dcol.at[k, half]

    def dr(f, d, half=None, other=False):
        k = cidx(f, d, other)
        return Drow.at[k] if half is None else Drow.at[k, half]

    def X(view, i, dev):
        push(view, xs.at[i], xr.at[i], dev)

    def Z(view, i, dev):
        push(view, zs.at[i], zr.at[i], dev)

    def to_twin(f, d):
        i = f * 4 + (d + 4) % 4
        push(dr(f, d), cs.at[i], cr.at[i], twin)

    def from_twin(f, d):
        got(dr(f, d, other=True), cr.at[f * 4 + (d + 4) % 4])

    X(dc(0, 0, 0), 0, ylod)
    X(dc(0, 0, 1), 1, ylod)
    X(dc(0, 0, 0), 2, xp)
    X(dc(0, 0, 1), 5, xm)
    Z(dr(0, 0, 0), 2, zp)
    Z(dr(0, 0, 1), 5, zm)
    X(dc(0, 0, 1), 3, xp)
    X(dc(0, 0, 0), 4, xm)
    Z(dr(0, 0, 1), 3, zp)
    Z(dr(0, 0, 0), 4, zm)
    to_twin(0, 0)

    def hp(q, f, d, half=None):
        k = ridx(f, d)
        return Hcol.at[q, k] if half is None else Hcol.at[q, k, half]

    H_OWN = ((0, 0, None, 0, ylod), (0, 0, None, 1, xp), (0, 0, None, 2, xm))
    H_MID = ((1, 0, None, 3, xp), (1, 0, None, 4, xm), (0, -1, 0, 5, xp), (0, 1, 1, 6, xm))
    H_FAR = ((1, -1, 0, 7, xp), (1, 1, 1, 8, xm))

    def h_push(q, f, d, half, i, dev):
        view = hp(q, f, d, half)
        remote(view, view, hs.at[q * 9 + i], hr.at[q * 9 + i], dev).start()

    def h_own(q):
        for a in H_OWN:
            h_push(q, *a)

    def h_mid(q):
        got(hp(q, 1, 0), hr.at[q * 9])
        h_push(q, *H_MID[0])
        h_push(q, *H_MID[1])
        got(hp(q, 0, -1), hr.at[q * 9 + 1])
        h_push(q, *H_MID[2])
        got(hp(q, 0, 1), hr.at[q * 9 + 2])
        h_push(q, *H_MID[3])

    def h_far(q):
        got(hp(q, 1, -1), hr.at[q * 9 + 3])
        h_push(q, *H_FAR[0])
        got(hp(q, 1, 1), hr.at[q * 9 + 4])
        h_push(q, *H_FAR[1])

    def h_end(q):
        got(hp(q, 0, 2, 0), hr.at[q * 9 + 5])
        got(hp(q, 0, 2, 1), hr.at[q * 9 + 6])
        got(hp(q, 1, 2, 0), hr.at[q * 9 + 7])
        got(hp(q, 1, 2, 1), hr.at[q * 9 + 8])

    def h_twin(q):
        remote(Hcol.at[q, :, 1 - core], Htw.at[q], ts.at[q], tr.at[q], twin).start()

    def spread(block, ind, store):
        for ii in range(4):
            b0, b1 = block(ii * 2), block(ii * 2 + 1)
            n = b0.shape[0] // 16
            for t in range(CB):
                k = ii * 8 + t
                i0 = jnp.broadcast_to(ind[k:k + 1], (16, BS)).astype(BF16)
                i1 = jnp.broadcast_to(ind[k + 4:k + 5], (16, BS)).astype(BF16)
                out = b0.reshape(n, 16, BS) * i0[None] + b1.reshape(n, 16, BS) * i1[None]
                store(ii, t, out.reshape(n * 16, BS))

    def spread_d(src, k, put):
        def body(half, carry):
            ind = src[k, half, pl.ds(HALF, IND), :].astype(F32)

            def store(ii, t, v):
                put(pl.ds(pl.multiple_of(half * 512 + ii * BS, BS), BS), t, v)

            spread(lambda b: src[k, half, pl.ds(b * BS, BS), :], ind, store)
            return carry
        lax.fori_loop(0, 2, body, 0)

    def put_r(at, t, v):
        Rd[at, pl.ds(t * BS, BS)] = v

    def panel(f, d, other):
        cc = (1 - core) if other else core
        k = cidx(f, d, other)

        def put(at, t, v):
            Dd[k // 2, at, pl.ds(pl.multiple_of(cc * COLS + t * BS, BS), BS)] = v
        spread_d(Drow, k, put)

    def panel2(f, d):
        from_twin(f, d)
        panel(f, d, True)

    def chunk(b, f, e):
        return (1 - ylo if f else ylo) * 4 + (b + e) % 4

    dz = (z - x + 4) % 4
    o0 = (dz // 2) * (1 - dz % 2)
    o1 = 1 + 2 * (dz // 2)
    o2 = 4 - o0 - o1
    odd = (ylo + yhi) % 2
    plain = [chunk(x, 0, e) for e in range(4)] + [chunk(x, 1, e) for e in (o0, o1, o2, 2)]
    mixed = [chunk(z, 0, 0), chunk(x, 1, 0), chunk(z, 0, 1), chunk(z, 0, 3),
             chunk(x, 1, 1), chunk(x, 1, 3), chunk(z, 0, 2), chunk(x, 1, 2)]
    chunks = [(1 - odd) * a + odd * b for a, b in zip(plain, mixed)]

    def products(n):
        def body(i, carry):
            k = chunks[n] + i * (chunks[n + 1] - chunks[n])
            spread_d(Dcol, k, put_r)
            accS[...] += jnp.dot(Dd[k], Rd[...], preferred_element_type=F32)
            return carry
        lax.fori_loop(0, 2, body, 0)

    accS[...] = jnp.zeros_like(accS)
    accM[...] = jnp.zeros_like(accM)
    for c in later:
        c.wait()
    panel(0, 0, False)

    def relay(h):
        got(dc(1, 0, h), xr.at[h])
        push(Dcol.at[ridx(1, 0), h, pl.ds(0, SH)], zs.at[h], zr.at[h], yind, Drow.at[col, h])

    relay(0)
    got(dc(0, -1, 0), xr.at[2])
    X(dc(0, -1, 0), 10, xp)
    got(dc(0, 1, 1), xr.at[5])
    X(dc(0, 1, 1), 11, xm)
    got(dr(0, -1, 0), zr.at[2])
    Z(dr(0, -1, 0), 10, zp)
    got(dr(0, 1, 1), zr.at[5])
    Z(dr(0, 1, 1), 11, zm)
    panel2(0, 0)
    relay(1)
    X(dc(1, 0, 0), 6, xp)
    X(dc(1, 0, 1), 9, xm)
    X(dc(1, 0, 1), 7, xp)
    X(dc(1, 0, 0), 8, xm)
    got(dr(0, -1, 1), zr.at[3])
    to_twin(0, -1)
    got(dr(0, 1, 0), zr.at[4])
    to_twin(0, 1)
    panel(0, -1, False)
    panel(0, 1, False)
    got(dr(1, 0, 0), zr.at[0])
    Z(dr(1, 0, 0), 6, zp)
    Z(dr(1, 0, 0), 8, zm)
    panel2(0, -1)
    panel2(0, 1)
    got(dr(0, 2, 0), zr.at[10])
    got(dr(0, 2, 1), zr.at[11])
    to_twin(0, 2)
    got(dr(1, 0, 1), zr.at[1])
    Z(dr(1, 0, 1), 7, zp)
    Z(dr(1, 0, 1), 9, zm)
    to_twin(1, 0)
    panel(0, 2, False)
    panel(1, 0, False)
    panel2(0, 2)
    panel2(1, 0)
    got(dc(0, -1, 1), xr.at[3])
    got(dc(0, 1, 0), xr.at[4])
    got(dc(0, 2, 0), xr.at[10])
    got(dc(0, 2, 1), xr.at[11])
    products(0)
    got(dc(1, -1, 0), xr.at[6])
    X(dc(1, -1, 0), 12, xp)
    got(dc(1, 1, 1), xr.at[9])
    X(dc(1, 1, 1), 13, xm)
    h_own(0)
    h_own(1)
    got(dr(1, -1, 0), zr.at[6])
    Z(dr(1, -1, 0), 12, zp)
    got(dr(1, 1, 1), zr.at[9])
    Z(dr(1, 1, 1), 13, zm)
    got(dr(1, -1, 1), zr.at[7])
    to_twin(1, -1)
    got(dr(1, 1, 0), zr.at[8])
    to_twin(1, 1)
    panel(1, -1, False)
    panel(1, 1, False)
    panel2(1, -1)
    panel2(1, 1)
    got(dc(1, -1, 1), xr.at[7])
    got(dc(1, 1, 0), xr.at[8])
    products(2)
    h_own(2)
    h_mid(0)
    products(4)
    got(dr(1, 2, 0), zr.at[12])
    got(dr(1, 2, 1), zr.at[13])
    to_twin(1, 2)
    got(dc(1, 2, 0), xr.at[12])
    got(dc(1, 2, 1), xr.at[13])
    h_mid(1)
    panel(1, 2, False)
    panel2(1, 2)
    h_own(3)
    h_far(0)
    products(6)

    Sown[...] = accS[...].astype(BF16)
    push(Sown, ts.at[NP], tr.at[NP], twin, Stw)
    push(Dcol.at[:, 1 - core, pl.ds(SH, IND)], ts.at[NP + 1], tr.at[NP + 1], twin, Hti)
    h_mid(2)
    h_own(4)
    h_end(0)
    h_twin(0)
    got(Stw, tr.at[NP])
    got(Hti, tr.at[NP + 1])

    def pick(acc, i, which):
        at = pl.ds(pl.multiple_of(i * BS, BS), BS)
        place = jnp.broadcast_to(which, (BS, BS))
        out = acc[at, pl.ds(0, BS)]
        for t in range(1, CB):
            out = jnp.where(place == t, acc[at, pl.ds(t * BS, BS)], out)
        return out

    def filtered(acc, out, i):
        for w in range(CB):
            out[i * CB + w] = pick(acc, i, filt[i, w:w + 1, :]).astype(BF16)

    NT = (((1,), (1,)), ((), ()))

    def partials(q):
        def rows(m, carry):
            def put(ref):
                def store(ii, t, v):
                    at = pl.ds(pl.multiple_of(m * 64 + ii * JP, JP), JP)
                    ref[at, pl.ds(t * BS, BS)] = v
                return store
            own = Dcol[m, core, pl.ds(SH, IND), :].astype(F32)
            spread(lambda b: Hcol[q, m, core, b], own, put(Hr0))
            spread(lambda b: Htw[q, m, b], Hti[m].astype(F32), put(Hr1))
            return carry
        lax.fori_loop(0, 8, rows, 0)
        CT[q % 2] = (
            lax.dot_general(Hr0[...], Sown[...], NT, preferred_element_type=F32)
            + lax.dot_general(Hr1[...], Stw[...], NT, preferred_element_type=F32)
        )

    def extract(q, m, half, emit):
        ind = Drow[2 * m + core, half, pl.ds(HALF, IND), :].astype(F32)
        for ii in range(4):
            lanes = pl.ds((half * 4 + ii) * BS, BS)
            v = [CT[q % 2, pl.ds(pl.multiple_of(m * 64 + t * JP, JP), JP), lanes] for t in range(CB)]
            for s in range(KS):
                out = v[0]
                for t in range(1, CB):
                    k = ii * 8 + s * 4 + t
                    hit = jnp.broadcast_to(ind[k:k + 1], (JP, BS)) > 0.5
                    out = jnp.where(hit, v[t], out)
                emit(ii * KS + s, out)

    def chip(f, d):
        hh = (1 - yhi) if f else yhi
        return hh * 4 + (z + d + 4) % 4

    def rs_far(q):
        for f in (1, 0):
            m = chip(f, 2)
            for half, (dev, dst) in enumerate(((zp, Al), (zm, Ar))):
                def emit(b, v, half=half):
                    PB[q, m, half * 8 + b] = v.astype(BF16)
                extract(q, m, half, emit)
                i = q * 4 + f * 2 + half
                remote(PB.at[q, m, pl.ds(half * 8, 8)], dst.at[q, f], as_.at[i], ar.at[i], dev).start()

    def rs_near(q):
        for f in (1, 0):
            for side, (d, dev, src, dst) in enumerate(((1, zp, Al, Bl), (-1, zm, Ar, Br))):
                m = chip(f, d)
                i = q * 4 + f * 2 + side
                got(src.at[q, f], ar.at[i])
                for half in (0, 1):
                    def emit(b, v, half=half):
                        if half == side:
                            v = v + src[q, f, b].astype(F32)
                        PB[q, m, half * 8 + b] = v.astype(BF16)
                    extract(q, m, half, emit)
                remote(PB.at[q, m], dst.at[q, f], bs.at[i], br.at[i], dev).start()

    def rs_keep(q):
        for f in (1, 0):
            for half in (0, 1):
                def emit(b, v, half=half):
                    OWN[q % 3, f, half * 8 + b] = v
                extract(q, chip(f, 0), half, emit)

    def rs_own(q):
        for f in (1, 0):
            m = chip(f, 0)
            got(Bl.at[q, f], br.at[q * 4 + f * 2])
            got(Br.at[q, f], br.at[q * 4 + f * 2 + 1])
            for b in range(RB * KS):
                v = OWN[q % 3, f, b] + Bl[q, f, b].astype(F32) + Br[q, f, b].astype(F32)
                if f:
                    PB[q, m, b] = v.astype(BF16)
                else:
                    cub[b, pl.ds(pl.multiple_of(q * JP, JP), JP), :] = v
            if f:
                remote(PB.at[q, m], Y.at[q], ys.at[q], yr.at[q], yhid).start()

    def m_chunk(k, carry):
        def body(half, c):
            ind = Dcol[k, half, pl.ds(SH, IND), :].astype(F32)

            def store(ii, t, v):
                Rd[pl.ds(pl.multiple_of(half * 512 + ii * BS, BS), BS), pl.ds(t * BS, BS)] = v

            spread(lambda b: Hcol[:, k, half, b].reshape(BS, BS), ind, store)
            return c
        lax.fori_loop(0, 2, body, 0)
        accM[...] += jnp.dot(Dd[k], Rd[...], preferred_element_type=F32)
        return carry

    def step(q, carry):
        @pl.when(q + 1 < NP)
        def _():
            h_far(q + 1)

        @pl.when(q + 3 < NP)
        def _():
            h_mid(q + 3)

        @pl.when(q + 5 < NP)
        def _():
            h_own(q + 5)

        @pl.when(q < NP)
        def _():
            filtered(accS, s_out, q)
            got(Htw.at[q], tr.at[q])
            partials(q)
            rs_far(q)

        @pl.when((q >= 1) & (q < NP + 1))
        def _():
            rs_near(q - 1)
            rs_keep(q - 1)

        @pl.when(q >= 3)
        def _():
            rs_own(q - 3)

        @pl.when(q + 1 < NP)
        def _():
            h_end(q + 1)
            h_twin(q + 1)

        @pl.when(q >= NP - 1)
        def _():
            lo = (q - NP + 1) * 2
            lax.fori_loop(lo, lo + 2, m_chunk, 0)

        return carry

    lax.fori_loop(0, NP + 3, step, 0)

    def m_rows(i, carry):
        filtered(accM, m_out, i)
        return carry

    lax.fori_loop(0, RB, m_rows, 0)

    def y_wait(q, carry):
        got(Y.at[q], yr.at[q])
        return carry

    lax.fori_loop(0, NP, y_wait, 0)

    def gradient(i, carry):
        for s in range(KS):
            b = i * KS + s
            cubic = cub[b] + Y[:, b].reshape(BS, BS).astype(F32)
            direct = pick(accM, i, dcols[i, s:s + 1, :])
            g_out[b] = (3.0 * direct - 2.0 * cubic.T).astype(BF16)
        return carry

    lax.fori_loop(0, RB, gradient, 0)

    for c in sends:
        c.wait_send()

    def drain(q, carry):
        for f, d, half, i, dev in H_OWN + H_MID + H_FAR:
            sent(hp(q, f, d, half), hs.at[q * 9 + i])
        sent(Htw.at[q], ts.at[q])
        for i in range(4):
            sent(Al.at[q, 0], as_.at[q * 4 + i])
            sent(Bl.at[q, 0], bs.at[q * 4 + i])
        sent(Y.at[q], ys.at[q])
        return carry

    lax.fori_loop(0, NP, drain, 0)


def local(density, density_cols, hamilton, hamilton_cols, filter_cols):
    base = lax.axis_index("col") * CB

    def indicators(cols):
        hit = cols[:, :, None] == base + jnp.arange(CB, dtype=jnp.int32)
        hit = jnp.broadcast_to(hit[..., None], (RB, KS, CB, BS))
        return hit.astype(BF16).reshape(2, IND, BS)

    def places(cols):
        return jnp.broadcast_to((cols - base)[:, :, None], cols.shape + (BS,))

    def values(v):
        return v.reshape(2, HALF, BS)

    hbm = pl.BlockSpec(memory_space=pl.ANY)
    vmem = pl.BlockSpec(memory_space=pltpu.VMEM)
    dma = lambda n: pltpu.SemaphoreType.DMA((n,))
    s, m, g = pl.pallas_call(
        kernel,
        out_shape=(
            jax.ShapeDtypeStruct((RB * CB, BS, BS), BF16),
            jax.ShapeDtypeStruct((RB * CB, BS, BS), BF16),
            jax.ShapeDtypeStruct((RB * KS, BS, BS), BF16),
        ),
        in_specs=[hbm] * 4 + [vmem] * 2,
        out_specs=(vmem,) * 3,
        scratch_shapes=[
            pltpu.VMEM((NR, 2, SH + IND, BS), BF16),
            pltpu.VMEM((NP, NR, 2, 8, JP, BS), BF16),
            pltpu.VMEM((NC, 2, SH, BS), BF16),
            pltpu.VMEM((NP, NR, 8, JP, BS), BF16),
            pltpu.VMEM((NR, IND, BS), BF16),
            pltpu.VMEM((ROWS, COLS), BF16),
            pltpu.VMEM((ROWS, COLS), BF16),
            pltpu.VMEM((NR, ROWS, CHUNK), BF16),
            pltpu.VMEM((CHUNK, COLS), BF16),
            pltpu.VMEM((NR * CB * JP, COLS), BF16),
            pltpu.VMEM((NR * CB * JP, COLS), BF16),
            pltpu.VMEM((ROWS, COLS), F32),
            pltpu.VMEM((ROWS, COLS), F32),
            pltpu.VMEM((2, NR * CB * JP, ROWS), F32),
            pltpu.VMEM((NP, NR, RB * KS, JP, BS), BF16),
            pltpu.VMEM((3, 2, RB * KS, JP, BS), F32),
            pltpu.VMEM((NP, 2, RB, JP, BS), BF16),
            pltpu.VMEM((NP, 2, RB, JP, BS), BF16),
            pltpu.VMEM((NP, 2, RB * KS, JP, BS), BF16),
            pltpu.VMEM((NP, 2, RB * KS, JP, BS), BF16),
            pltpu.VMEM((NP, RB * KS, JP, BS), BF16),
            pltpu.VMEM((RB * KS, BS, BS), F32),
            dma(5 + NP), dma(14), dma(14), dma(14), dma(14), dma(9 * NP), dma(9 * NP),
            dma(8), dma(8), dma(NP + 2), dma(NP + 2), dma(4 * NP), dma(4 * NP),
            dma(4 * NP), dma(4 * NP), dma(NP), dma(NP),
        ],
        compiler_params=pltpu.CompilerParams(
            collective_id=0, has_side_effects=True, vmem_limit_bytes=67_000_000),
    )(values(density), indicators(density_cols),
      hamilton.reshape(2, 8, NP, JP, BS),
      indicators(hamilton_cols), places(filter_cols), places(density_cols))
    return (s.reshape(RB, CB, BS, BS), m.reshape(RB, CB, BS, BS), g.reshape(RB, KS, BS, BS))


def solution(mesh):
    blocks, cols = P("row", "col", None, None), P("row", "col")
    return jax.shard_map(
        local, mesh=mesh, in_specs=(blocks, cols, blocks, cols, cols),
        out_specs=(blocks,) * 3, check_vma=False)
```

```python
import jax
import jax.numpy as jnp
from jax import lax
from jax.experimental import pallas as pl
from jax.experimental.pallas import tpu as pltpu
from jax.sharding import PartitionSpec as P

MESH = pl.DeviceIdType.MESH
BF16, F32 = jnp.bfloat16, jnp.float32
BS = 128
RB, CB = 8, 4
NR, NC = 8, 16
KS = 2
HALF = 4 * KS * BS
IND = 4 * KS * CB
SH = HALF + IND
NP = 8
JP = BS // NP
HS = 8
ROWS, COLS, CHUNK = RB * BS, CB * BS, RB * BS


def remote(src, dst, send, recv, dev):
    return pltpu.make_async_remote_copy(
        src_ref=src, dst_ref=dst, send_sem=send, recv_sem=recv,
        device_id=dev, device_id_type=MESH,
    )


def kernel(dv, hv, dcols, hcols, s_out, m_out, g_out,
           Dcol, Hcol, Drow, Htw, Hti, Sown, Stw, Mout, Dd, Rd, Hr0, Hr1, accS, accM, CT,
           PB, OWN, Al, Ar, Bl, Br, Y, cub,
           loc, xs, xr, zs, zr, hs, hr, cs, cr, ts, tr, as_, ar, bs, br, ys, yr):
    row, col = lax.axis_index("row"), lax.axis_index("col")
    x, ylo = row % 4, row // 4
    core, z, yhi = col % 2, (col // 2) % 4, col // 8

    def ridx(f, d):
        yy = (1 - ylo) if f else ylo
        return yy * 4 + (x + d + 4) % 4

    def cidx(f, d, other=False):
        yy = (1 - yhi) if f else yhi
        cc = (1 - core) if other else core
        return yy * 8 + ((z + d + 4) % 4) * 2 + cc

    xp, xm = (ridx(0, 1), col), (ridx(0, -1), col)
    zp, zm = (row, cidx(0, 1)), (row, cidx(0, -1))
    ylod = (ridx(1, 0), col)
    yind = (ridx(1, 0), cidx(1, 0))
    yhid = (row, cidx(1, 0))
    twin = (row, cidx(0, 0, True))

    first = [
        pltpu.make_async_copy(dv, Dcol.at[row, :, pl.ds(0, HALF), :], loc.at[0]),
        pltpu.make_async_copy(dv, Drow.at[col, :, pl.ds(0, HALF), :], loc.at[1]),
    ]
    later = [
        pltpu.make_async_copy(hv.at[:, :, q], Hcol.at[q, row], loc.at[2 + q])
        for q in range(NP)
    ]
    for c in first + later:
        c.start()
    barrier = pltpu.get_barrier_semaphore()
    for dev in (xp, xm, zp, zm, ylod, yind, yhid, twin):
        pl.semaphore_signal(barrier, inc=1, device_id=dev, device_id_type=MESH)

    line = lax.broadcasted_iota(jnp.int32, (IND, BS), 0)

    def indicators(cols, half):
        place = jnp.zeros((IND, BS), jnp.int32)
        for ii in range(4):
            for s in range(KS):
                c = jnp.full((IND, BS), cols[half * 4 + ii, s] - col * CB, jnp.int32)
                place = jnp.where(line // CB == ii * KS + s, c, place)
        return jnp.where(place == line % CB, 1.0, 0.0).astype(BF16)

    for half in (0, 1):
        ind = indicators(dcols, half)
        Dcol[row, half, pl.ds(HALF, IND), :] = ind
        Drow[col, half, pl.ds(HALF, IND), :] = ind
        Dcol[row, half, pl.ds(SH, IND), :] = indicators(hcols, half)
    for c in first:
        c.wait()
    pl.semaphore_wait(barrier, 8)

    sends = []

    def push(view, send, recv, dev, there=None):
        c = remote(view, view if there is None else there, send, recv, dev)
        c.start()
        sends.append(c)

    def got(view, recv):
        remote(view, view, recv, recv, twin).wait_recv()

    def sent(view, send):
        remote(view, view, send, send, twin).wait_send()

    def dc(f, d, half=None):
        k = ridx(f, d)
        return Dcol.at[k] if half is None else Dcol.at[k, half]

    def dr(f, d, half=None, other=False):
        k = cidx(f, d, other)
        return Drow.at[k] if half is None else Drow.at[k, half]

    def quarter(f, d, part):
        return Drow.at[cidx(f, d), 0, pl.ds(part * (SH // 2), SH // 2)]

    def X(view, i, dev):
        push(view, xs.at[i], xr.at[i], dev)

    def Z(view, i, dev):
        push(view, zs.at[i], zr.at[i], dev)

    def to_twin(f, d):
        i = f * 4 + (d + 4) % 4
        push(dr(f, d), cs.at[i], cr.at[i], twin)

    def from_twin(f, d):
        got(dr(f, d, other=True), cr.at[f * 4 + (d + 4) % 4])

    X(dc(0, 0, 0), 0, ylod)
    X(dc(0, 0, 1), 1, ylod)
    X(dc(0, 0, 0), 2, xp)
    X(dc(0, 0, 1), 5, xm)
    Z(dr(0, 0, 0), 2, zp)
    Z(dr(0, 0, 1), 5, zm)
    X(dc(0, 0, 1), 3, xp)
    X(dc(0, 0, 0), 4, xm)
    Z(dr(0, 0, 1), 3, zp)
    Z(dr(0, 0, 0), 4, zm)
    to_twin(0, 0)

    def hp(q, f, d, half=None):
        k = ridx(f, d)
        return Hcol.at[q, k] if half is None else Hcol.at[q, k, half]

    H_OWN = ((0, 0, None, 0, ylod), (0, 0, None, 1, xp), (0, 0, None, 2, xm))
    H_MID = ((0, -1, 0, 5, xp), (0, 1, 1, 6, xm), (1, 0, None, 3, xp), (1, 0, None, 4, xm))
    H_FAR = ((0, 2, None, 7, ylod),)

    def h_push(q, f, d, half, i, dev):
        view = hp(q, f, d, half)
        remote(view, view, hs.at[q * HS + i], hr.at[q * HS + i], dev).start()

    def h_own(q):
        for a in H_OWN:
            h_push(q, *a)

    def h_mid(q):
        got(hp(q, 0, -1), hr.at[q * HS + 1])
        h_push(q, *H_MID[0])
        got(hp(q, 0, 1), hr.at[q * HS + 2])
        h_push(q, *H_MID[1])
        got(hp(q, 1, 0), hr.at[q * HS])
        h_push(q, *H_MID[2])
        h_push(q, *H_MID[3])

    def h_far(q):
        got(hp(q, 0, 2, 0), hr.at[q * HS + 5])
        got(hp(q, 0, 2, 1), hr.at[q * HS + 6])
        h_push(q, *H_FAR[0])

    def h_end(q):
        got(hp(q, 1, -1), hr.at[q * HS + 3])
        got(hp(q, 1, 1), hr.at[q * HS + 4])
        got(hp(q, 1, 2), hr.at[q * HS + 7])

    def h_twin(q):
        remote(Hcol.at[q, :, 1 - core], Htw.at[q], ts.at[q], tr.at[q], twin).start()

    def spread(block, ind, store):
        for ii in range(4):
            b0, b1 = block(ii * 2), block(ii * 2 + 1)
            n = b0.shape[0] // 16
            for t in range(CB):
                k = ii * 8 + t
                i0 = jnp.broadcast_to(ind[k:k + 1], (16, BS)).astype(BF16)
                i1 = jnp.broadcast_to(ind[k + 4:k + 5], (16, BS)).astype(BF16)
                out = b0.reshape(n, 16, BS) * i0[None] + b1.reshape(n, 16, BS) * i1[None]
                store(ii, t, out.reshape(n * 16, BS))

    def spread_d(src, k, put):
        def body(half, carry):
            ind = src[k, half, pl.ds(HALF, IND), :].astype(F32)

            def store(ii, t, v):
                put(pl.ds(pl.multiple_of(half * 512 + ii * BS, BS), BS), t, v)

            spread(lambda b: src[k, half, pl.ds(b * BS, BS), :], ind, store)
            return carry
        lax.fori_loop(0, 2, body, 0)

    def put_r(at, t, v):
        Rd[at, pl.ds(t * BS, BS)] = v

    def panel(f, d, other):
        cc = (1 - core) if other else core
        k = cidx(f, d, other)

        def put(at, t, v):
            Dd[k // 2, at, pl.ds(pl.multiple_of(cc * COLS + t * BS, BS), BS)] = v
        spread_d(Drow, k, put)

    def panel2(f, d):
        from_twin(f, d)
        panel(f, d, True)

    def chunk(b, f, e):
        return (1 - ylo if f else ylo) * 4 + (b + e) % 4

    dz = (z - x + 4) % 4
    o0 = (dz // 2) * (1 - dz % 2)
    o1 = 1 + 2 * (dz // 2)
    o2 = 4 - o0 - o1
    odd = (ylo + yhi) % 2
    plain = [chunk(x, 0, e) for e in range(4)] + [chunk(x, 1, e) for e in (o0, o1, o2 + 2 - (dz + 2) % 4, (dz + 2) % 4)]
    mixed = [chunk(z, 0, 0), chunk(x, 1, 0), chunk(z, 0, 1), chunk(z, 0, 3),
             chunk(x, 1, 1), chunk(x, 1, 3), chunk(x, 1, 2), chunk(z, 0, 2)]
    chunks = [(1 - odd) * a + odd * b for a, b in zip(plain, mixed)]

    def product(k):
        spread_d(Dcol, k, put_r)
        accS[...] += jnp.dot(Dd[k], Rd[...], preferred_element_type=F32)

    def products(n):
        def body(i, carry):
            product(chunks[n] + i * (chunks[n + 1] - chunks[n]))
            return carry
        lax.fori_loop(0, 2, body, 0)

    accS[...] = jnp.zeros_like(accS)
    accM[...] = jnp.zeros_like(accM)
    for c in later:
        c.wait()
    panel(0, 0, False)

    def relay(h):
        got(dc(1, 0, h), xr.at[h])
        push(Dcol.at[ridx(1, 0), h, pl.ds(0, SH)], zs.at[h], zr.at[h], yind, Drow.at[col, h])

    relay(0)
    got(dc(0, -1, 0), xr.at[2])
    X(dc(0, -1, 0), 10, xp)
    got(dc(0, 1, 1), xr.at[5])
    X(dc(0, 1, 1), 11, xm)
    got(dr(0, -1, 0), zr.at[2])
    Z(dr(0, -1, 0), 10, zp)
    got(dr(0, 1, 1), zr.at[5])
    Z(dr(0, 1, 1), 11, zm)
    panel2(0, 0)
    relay(1)
    X(dc(1, 0, 0), 6, xp)
    X(dc(1, 0, 1), 9, xm)
    X(dc(1, 0, 1), 7, xp)
    X(dc(1, 0, 0), 8, xm)
    h_own(0)
    h_own(1)
    h_own(2)
    got(dr(0, -1, 1), zr.at[3])
    to_twin(0, -1)
    got(dr(0, 1, 0), zr.at[4])
    to_twin(0, 1)
    panel(0, -1, False)
    panel(0, 1, False)
    got(dr(1, 0, 0), zr.at[0])
    Z(dr(1, 0, 0), 6, zp)
    Z(dr(1, 0, 0), 8, zm)
    panel2(0, -1)
    panel2(0, 1)
    got(dc(0, 2, 0), xr.at[10])
    X(dc(0, 2, 0), 12, ylod)
    got(dc(0, 2, 1), xr.at[11])
    X(dc(0, 2, 1), 13, ylod)
    got(dr(0, 2, 0), zr.at[10])
    got(dr(0, 2, 1), zr.at[11])
    Z(dr(0, 2, 1), 14, yhid)
    to_twin(0, 2)
    got(dr(1, 0, 1), zr.at[1])
    Z(dr(1, 0, 1), 7, zp)
    Z(dr(1, 0, 1), 9, zm)
    to_twin(1, 0)
    panel(0, 2, False)
    panel(1, 0, False)
    panel2(0, 2)
    panel2(1, 0)
    got(dc(0, -1, 1), xr.at[3])
    got(dc(0, 1, 0), xr.at[4])
    products(0)
    got(dr(1, -1, 0), zr.at[6])
    Z(quarter(1, -1, 0), 12, zp)
    got(dr(1, 1, 0), zr.at[8])
    Z(quarter(1, 1, 1), 13, zm)
    got(dr(1, -1, 1), zr.at[7])
    to_twin(1, -1)
    got(dr(1, 1, 1), zr.at[9])
    to_twin(1, 1)
    panel(1, -1, False)
    panel(1, 1, False)
    panel2(1, -1)
    panel2(1, 1)
    got(dc(1, -1, 0), xr.at[6])
    got(dc(1, 1, 1), xr.at[9])
    got(dc(1, -1, 1), xr.at[7])
    got(dc(1, 1, 0), xr.at[8])
    products(2)
    h_mid(0)
    h_own(3)
    products(4)
    got(dc(1, 2, 0), xr.at[12])
    got(dc(1, 2, 1), xr.at[13])
    push(Dcol.at[:, 1 - core, pl.ds(SH, IND)], ts.at[NP + 1], tr.at[NP + 1], twin, Hti)
    got(quarter(1, 2, 0), zr.at[12])
    got(quarter(1, 2, 1), zr.at[13])
    got(dr(1, 2, 1), zr.at[14])
    to_twin(1, 2)
    h_mid(1)
    h_far(0)
    h_own(4)
    product(chunks[6])
    panel(1, 2, False)
    panel2(1, 2)
    product(chunks[7])

    Sown[...] = accS[...].astype(BF16)
    push(Sown, ts.at[NP], tr.at[NP], twin, Stw)
    h_mid(2)
    h_far(1)
    h_own(5)
    h_end(0)
    h_twin(0)
    out_s = pltpu.make_async_copy(Sown, s_out, loc.at[0])
    out_s.start()
    got(Hti, tr.at[NP + 1])

    def pick(acc, i, which):
        at = pl.ds(pl.multiple_of(i * BS, BS), BS)
        place = jnp.full((BS, BS), which, jnp.int32)
        out = acc[at, pl.ds(0, BS)]
        for t in range(1, CB):
            out = jnp.where(place == t, acc[at, pl.ds(t * BS, BS)], out)
        return out

    NT = (((1,), (1,)), ((), ()))

    def partials(q):
        def rows(m, carry):
            def put(ref):
                def store(ii, t, v):
                    at = pl.ds(pl.multiple_of(m * 64 + ii * JP, JP), JP)
                    ref[at, pl.ds(t * BS, BS)] = v
                return store
            own = Dcol[m, core, pl.ds(SH, IND), :].astype(F32)
            spread(lambda b: Hcol[q, m, core, b], own, put(Hr0))
            spread(lambda b: Htw[q, m, b], Hti[m].astype(F32), put(Hr1))
            return carry
        lax.fori_loop(0, 8, rows, 0)

        @pl.when(q == 0)
        def _():
            got(Stw, tr.at[NP])

        CT[q % 2] = (
            lax.dot_general(Hr0[...], Sown[...], NT, preferred_element_type=F32)
            + lax.dot_general(Hr1[...], Stw[...], NT, preferred_element_type=F32)
        )

    def extract(q, m, half, emit):
        ind = Drow[2 * m + core, half, pl.ds(HALF, IND), :].astype(F32)
        for ii in range(4):
            lanes = pl.ds((half * 4 + ii) * BS, BS)
            v = [CT[q % 2, pl.ds(pl.multiple_of(m * 64 + t * JP, JP), JP), lanes] for t in range(CB)]
            for s in range(KS):
                out = v[0]
                for t in range(1, CB):
                    k = ii * 8 + s * 4 + t
                    hit = jnp.broadcast_to(ind[k:k + 1], (JP, BS)) > 0.5
                    out = jnp.where(hit, v[t], out)
                emit(ii * KS + s, out)

    def chip(f, d):
        hh = (1 - yhi) if f else yhi
        return hh * 4 + (z + d + 4) % 4

    def rs_far(q):
        for f in (1, 0):
            m = chip(f, 2)
            for half, (dev, dst) in enumerate(((zp, Al), (zm, Ar))):
                def emit(b, v, half=half):
                    PB[q, m, half * 8 + b] = v.astype(BF16)
                extract(q, m, half, emit)
                i = q * 4 + f * 2 + half
                remote(PB.at[q, m, pl.ds(half * 8, 8)], dst.at[q, f], as_.at[i], ar.at[i], dev).start()

    def rs_near(q):
        for f in (1, 0):
            for side, (d, dev, src, dst) in enumerate(((1, zp, Al, Bl), (-1, zm, Ar, Br))):
                m = chip(f, d)
                i = q * 4 + f * 2 + side
                got(src.at[q, f], ar.at[i])
                for half in (0, 1):
                    def emit(b, v, half=half):
                        if half == side:
                            v = v + src[q, f, b].astype(F32)
                        PB[q, m, half * 8 + b] = v.astype(BF16)
                    extract(q, m, half, emit)
                remote(PB.at[q, m], dst.at[q, f], bs.at[i], br.at[i], dev).start()

    def rs_keep(q):
        for f in (1, 0):
            for half in (0, 1):
                def emit(b, v, half=half):
                    OWN[q % 3, f, half * 8 + b] = v
                extract(q, chip(f, 0), half, emit)

    def rs_own(q):
        for f in (1, 0):
            m = chip(f, 0)
            got(Bl.at[q, f], br.at[q * 4 + f * 2])
            got(Br.at[q, f], br.at[q * 4 + f * 2 + 1])
            for b in range(RB * KS):
                v = OWN[q % 3, f, b] + Bl[q, f, b].astype(F32) + Br[q, f, b].astype(F32)
                if f:
                    PB[q, m, b] = v.astype(BF16)
                else:
                    cub[b, pl.ds(pl.multiple_of(q * JP, JP), JP), :] = v
            if f:
                remote(PB.at[q, m], Y.at[q], ys.at[q], yr.at[q], yhid).start()

    def m_chunk(k, carry):
        def body(half, c):
            ind = Dcol[k, half, pl.ds(SH, IND), :].astype(F32)

            def store(ii, t, v):
                Rd[pl.ds(pl.multiple_of(half * 512 + ii * BS, BS), BS), pl.ds(t * BS, BS)] = v

            spread(lambda b: Hcol[:, k, half, b].reshape(BS, BS), ind, store)
            return c
        lax.fori_loop(0, 2, body, 0)
        accM[...] += jnp.dot(Dd[k], Rd[...], preferred_element_type=F32)
        return carry

    def step(q, carry):
        @pl.when(q + 2 < NP)
        def _():
            h_far(q + 2)

        @pl.when(q + 3 < NP)
        def _():
            h_mid(q + 3)

        @pl.when(q + 6 < NP)
        def _():
            h_own(q + 6)

        @pl.when(q < NP)
        def _():
            got(Htw.at[q], tr.at[q])
            partials(q)
            rs_far(q)

        @pl.when((q >= 1) & (q < NP + 1))
        def _():
            rs_near(q - 1)
            rs_keep(q - 1)

        @pl.when(q >= 3)
        def _():
            rs_own(q - 3)

        @pl.when(q + 1 < NP)
        def _():
            h_end(q + 1)
            h_twin(q + 1)

        @pl.when(q >= NP - 1)
        def _():
            lo = (q - NP + 1) * 2
            lax.fori_loop(lo, lo + 2, m_chunk, 0)

        return carry

    lax.fori_loop(0, NP + 3, step, 0)

    Mout[...] = accM[...].astype(BF16)
    out_m = pltpu.make_async_copy(Mout, m_out, loc.at[1])
    out_m.start()

    def y_wait(q, carry):
        got(Y.at[q], yr.at[q])
        return carry

    lax.fori_loop(0, NP, y_wait, 0)

    def gradient(i, carry):
        for s in range(KS):
            b = i * KS + s
            cubic = cub[b] + Y[:, b].reshape(BS, BS).astype(F32)
            direct = pick(accM, i, dcols[i, s] - col * CB)
            g_out[b] = (3.0 * direct - 2.0 * cubic.T).astype(BF16)
        return carry

    lax.fori_loop(0, RB, gradient, 0)
    out_s.wait()
    out_m.wait()

    for c in sends:
        c.wait_send()

    def drain(q, carry):
        for f, d, half, i, dev in H_OWN + H_MID + H_FAR:
            sent(hp(q, f, d, half), hs.at[q * HS + i])
        sent(Htw.at[q], ts.at[q])
        for i in range(4):
            sent(Al.at[q, 0], as_.at[q * 4 + i])
            sent(Bl.at[q, 0], bs.at[q * 4 + i])
        sent(Y.at[q], ys.at[q])
        return carry

    lax.fori_loop(0, NP, drain, 0)


def place_kernel(filt, s_in, m_in, g_in, s_out, m_out, g_out, sv, mv, gv, came, went):
    base = lax.axis_index("col") * CB
    ins = [pltpu.make_async_copy(a, v, came.at[n])
           for n, (a, v) in enumerate(((s_in, sv), (m_in, mv), (g_in, gv)))]
    for c in ins:
        c.start()
    outs = []
    for n, (v, out) in enumerate(((sv, s_out), (mv, m_out))):
        ins[n].wait()
        for i in range(RB):
            for w in range(CB):
                lanes = pl.ds(pl.multiple_of((filt[i, w] - base) * BS, BS), BS)
                k = i * CB + w
                c = pltpu.make_async_copy(
                    v.at[pl.ds(i * BS, BS), lanes], out.at[k], went.at[n * RB * CB + k])
                c.start()
                outs.append(c)
    ins[2].wait()
    c = pltpu.make_async_copy(gv, g_out, went.at[2 * RB * CB])
    c.start()
    for c in outs + [c]:
        c.wait()


def local(density, density_cols, hamilton, hamilton_cols, filter_cols):
    hbm = pl.BlockSpec(memory_space=pl.ANY)
    vmem = pl.BlockSpec(memory_space=pltpu.VMEM)
    smem = pl.BlockSpec(memory_space=pltpu.SMEM)
    dma = lambda n: pltpu.SemaphoreType.DMA((n,))
    s, m, g = pl.pallas_call(
        kernel,
        out_shape=(
            jax.ShapeDtypeStruct((ROWS, COLS), BF16),
            jax.ShapeDtypeStruct((ROWS, COLS), BF16),
            jax.ShapeDtypeStruct((RB * KS, BS, BS), BF16),
        ),
        in_specs=[hbm] * 2 + [smem] * 2,
        out_specs=(hbm, hbm, vmem),
        scratch_shapes=[
            pltpu.VMEM((NR, 2, SH + IND, BS), BF16),
            pltpu.VMEM((NP, NR, 2, 8, JP, BS), BF16),
            pltpu.VMEM((NC, 2, SH, BS), BF16),
            pltpu.VMEM((NP, NR, 8, JP, BS), BF16),
            pltpu.VMEM((NR, IND, BS), BF16),
            pltpu.VMEM((ROWS, COLS), BF16),
            pltpu.VMEM((ROWS, COLS), BF16),
            pltpu.VMEM((ROWS, COLS), BF16),
            pltpu.VMEM((NR, ROWS, CHUNK), BF16),
            pltpu.VMEM((CHUNK, COLS), BF16),
            pltpu.VMEM((NR * CB * JP, COLS), BF16),
            pltpu.VMEM((NR * CB * JP, COLS), BF16),
            pltpu.VMEM((ROWS, COLS), F32),
            pltpu.VMEM((ROWS, COLS), F32),
            pltpu.VMEM((2, NR * CB * JP, ROWS), F32),
            pltpu.VMEM((NP, NR, RB * KS, JP, BS), BF16),
            pltpu.VMEM((3, 2, RB * KS, JP, BS), F32),
            pltpu.VMEM((NP, 2, RB, JP, BS), BF16),
            pltpu.VMEM((NP, 2, RB, JP, BS), BF16),
            pltpu.VMEM((NP, 2, RB * KS, JP, BS), BF16),
            pltpu.VMEM((NP, 2, RB * KS, JP, BS), BF16),
            pltpu.VMEM((NP, RB * KS, JP, BS), BF16),
            pltpu.VMEM((RB * KS, BS, BS), F32),
            dma(2 + NP), dma(14), dma(14), dma(15), dma(15), dma(HS * NP), dma(HS * NP),
            dma(8), dma(8), dma(NP + 2), dma(NP + 2), dma(4 * NP), dma(4 * NP),
            dma(4 * NP), dma(4 * NP), dma(NP), dma(NP),
        ],
        compiler_params=pltpu.CompilerParams(
            collective_id=0, has_side_effects=True, vmem_limit_bytes=67_000_000),
    )(density.reshape(2, HALF, BS), hamilton.reshape(2, 8, NP, JP, BS), density_cols, hamilton_cols)
    slots = jax.ShapeDtypeStruct((RB * CB, BS, BS), BF16)
    s, m, g = pl.pallas_call(
        place_kernel,
        out_shape=(slots, slots, jax.ShapeDtypeStruct((RB * KS, BS, BS), BF16)),
        in_specs=[smem] + [hbm] * 3,
        out_specs=(hbm,) * 3,
        scratch_shapes=[
            pltpu.VMEM((ROWS, COLS), BF16),
            pltpu.VMEM((ROWS, COLS), BF16),
            pltpu.VMEM((RB * KS, BS, BS), BF16),
            dma(3), dma(2 * RB * CB + 1),
        ],
    )(filter_cols, s, m, g)
    return (s.reshape(RB, CB, BS, BS), m.reshape(RB, CB, BS, BS), g.reshape(RB, KS, BS, BS))


def solution(mesh):
    blocks, cols = P("row", "col", None, None), P("row", "col")
    return jax.shard_map(
        local, mesh=mesh, in_specs=(blocks, cols, blocks, cols, cols),
        out_specs=(blocks,) * 3, check_vma=False)
```

```python
import jax
import jax.numpy as jnp
from jax import lax
from jax.experimental import pallas as pl
from jax.experimental.pallas import tpu as pltpu
from jax.sharding import PartitionSpec as P

MESH = pl.DeviceIdType.MESH
BF16, F32 = jnp.bfloat16, jnp.float32
BS = 128
RB, CB = 8, 4
NR, NC = 8, 16
KS = 2
HALF = 4 * KS * BS
IND = 4 * KS * CB
SH = HALF + IND
NP = 8
JP = BS // NP
HS = 8
ROWS, COLS, CHUNK = RB * BS, CB * BS, RB * BS


def remote(src, dst, send, recv, dev):
    return pltpu.make_async_remote_copy(
        src_ref=src, dst_ref=dst, send_sem=send, recv_sem=recv,
        device_id=dev, device_id_type=MESH,
    )


def kernel(dv, hv, dcols, hcols, s_out, m_out, g_out,
           Dcol, Hcol, Drow, Htw, Hti, Sown, Stw, Mout, Dd, Rd, Hr0, Hr1, accS, accM, CT,
           PB, OWN, Al, Ar, Bl, Br, Y, cub,
           loc, xs, xr, zs, zr, hs, hr, cs, cr, ts, tr, as_, ar, bs, br, ys, yr):
    row, col = lax.axis_index("row"), lax.axis_index("col")
    x, ylo = row % 4, row // 4
    core, z, yhi = col % 2, (col // 2) % 4, col // 8

    def ridx(f, d):
        yy = (1 - ylo) if f else ylo
        return yy * 4 + (x + d + 4) % 4

    def cidx(f, d, other=False):
        yy = (1 - yhi) if f else yhi
        cc = (1 - core) if other else core
        return yy * 8 + ((z + d + 4) % 4) * 2 + cc

    xp, xm = (ridx(0, 1), col), (ridx(0, -1), col)
    zp, zm = (row, cidx(0, 1)), (row, cidx(0, -1))
    ylod = (ridx(1, 0), col)
    yind = (ridx(1, 0), cidx(1, 0))
    yhid = (row, cidx(1, 0))
    twin = (row, cidx(0, 0, True))

    first = [
        pltpu.make_async_copy(dv, Dcol.at[row, :, pl.ds(0, HALF), :], loc.at[0]),
        pltpu.make_async_copy(dv, Drow.at[col, :, pl.ds(0, HALF), :], loc.at[1]),
    ]
    later = [
        pltpu.make_async_copy(hv.at[:, :, q], Hcol.at[q, row], loc.at[2 + q])
        for q in range(NP)
    ]
    for c in first + later:
        c.start()
    barrier = pltpu.get_barrier_semaphore()
    for dev in (xp, xm, zp, zm, ylod, yind, yhid, twin):
        pl.semaphore_signal(barrier, inc=1, device_id=dev, device_id_type=MESH)

    line = lax.broadcasted_iota(jnp.int32, (IND, BS), 0)

    def indicators(cols, half):
        place = jnp.zeros((IND, BS), jnp.int32)
        for ii in range(4):
            for s in range(KS):
                c = jnp.full((IND, BS), cols[s, half * 4 + ii] - col * CB, jnp.int32)
                place = jnp.where(line // CB == ii * KS + s, c, place)
        return jnp.where(place == line % CB, 1.0, 0.0).astype(BF16)

    for half in (0, 1):
        ind = indicators(dcols, half)
        Dcol[row, half, pl.ds(HALF, IND), :] = ind
        Drow[col, half, pl.ds(HALF, IND), :] = ind
        Dcol[row, half, pl.ds(SH, IND), :] = indicators(hcols, half)
    for c in first:
        c.wait()
    pl.semaphore_wait(barrier, 8)

    sends = []

    def push(view, send, recv, dev, there=None):
        c = remote(view, view if there is None else there, send, recv, dev)
        c.start()
        sends.append(c)

    def got(view, recv):
        remote(view, view, recv, recv, twin).wait_recv()

    def sent(view, send):
        remote(view, view, send, send, twin).wait_send()

    def dc(f, d, half=None):
        k = ridx(f, d)
        return Dcol.at[k] if half is None else Dcol.at[k, half]

    def dr(f, d, half=None, other=False):
        k = cidx(f, d, other)
        return Drow.at[k] if half is None else Drow.at[k, half]

    def X(view, i, dev):
        push(view, xs.at[i], xr.at[i], dev)

    def Z(view, i, dev):
        push(view, zs.at[i], zr.at[i], dev)

    def to_twin(f, d):
        i = f * 4 + (d + 4) % 4
        push(dr(f, d), cs.at[i], cr.at[i], twin)

    def from_twin(f, d):
        got(dr(f, d, other=True), cr.at[f * 4 + (d + 4) % 4])

    X(dc(0, 0, 0), 0, ylod)
    X(dc(0, 0, 1), 1, ylod)
    X(dc(0, 0, 0), 2, xp)
    X(dc(0, 0, 1), 5, xm)
    Z(dr(0, 0, 0), 2, zp)
    Z(dr(0, 0, 1), 5, zm)
    X(dc(0, 0, 1), 3, xp)
    X(dc(0, 0, 0), 4, xm)
    Z(dr(0, 0, 1), 3, zp)
    Z(dr(0, 0, 0), 4, zm)
    to_twin(0, 0)

    def hp(q, f, d, half=None):
        k = ridx(f, d)
        return Hcol.at[q, k] if half is None else Hcol.at[q, k, half]

    H_OWN = ((0, 0, None, 0, ylod), (0, 0, None, 1, xp), (0, 0, None, 2, xm))
    H_MID = ((0, -1, 0, 5, xp), (0, 1, 1, 6, xm), (1, 0, None, 3, xp), (1, 0, None, 4, xm))
    H_FAR = ((0, 2, None, 7, ylod),)

    def h_push(q, f, d, half, i, dev):
        view = hp(q, f, d, half)
        remote(view, view, hs.at[q * HS + i], hr.at[q * HS + i], dev).start()

    def h_own(q):
        for a in H_OWN:
            h_push(q, *a)

    def h_mid(q):
        got(hp(q, 0, -1), hr.at[q * HS + 1])
        h_push(q, *H_MID[0])
        got(hp(q, 0, 1), hr.at[q * HS + 2])
        h_push(q, *H_MID[1])
        got(hp(q, 1, 0), hr.at[q * HS])
        h_push(q, *H_MID[2])
        h_push(q, *H_MID[3])

    def h_far(q):
        got(hp(q, 0, 2, 0), hr.at[q * HS + 5])
        got(hp(q, 0, 2, 1), hr.at[q * HS + 6])
        h_push(q, *H_FAR[0])

    def h_end(q):
        got(hp(q, 1, -1), hr.at[q * HS + 3])
        got(hp(q, 1, 1), hr.at[q * HS + 4])
        got(hp(q, 1, 2), hr.at[q * HS + 7])

    def h_twin(q):
        remote(Hcol.at[q, :, 1 - core], Htw.at[q], ts.at[q], tr.at[q], twin).start()

    def spread(block, ind, store):
        for ii in range(4):
            b0, b1 = block(ii * 2), block(ii * 2 + 1)
            n = b0.shape[0] // 16
            for t in range(CB):
                k = ii * 8 + t
                i0 = jnp.broadcast_to(ind[k:k + 1], (16, BS)).astype(BF16)
                i1 = jnp.broadcast_to(ind[k + 4:k + 5], (16, BS)).astype(BF16)
                out = b0.reshape(n, 16, BS) * i0[None] + b1.reshape(n, 16, BS) * i1[None]
                store(ii, t, out.reshape(n * 16, BS))

    def spread_d(src, k, put):
        def body(half, carry):
            ind = src[k, half, pl.ds(HALF, IND), :].astype(F32)

            def store(ii, t, v):
                put(pl.ds(pl.multiple_of(half * 512 + ii * BS, BS), BS), t, v)

            spread(lambda b: src[k, half, pl.ds(b * BS, BS), :], ind, store)
            return carry
        lax.fori_loop(0, 2, body, 0)

    def put_r(at, t, v):
        Rd[at, pl.ds(t * BS, BS)] = v

    def panel(f, d, other):
        cc = (1 - core) if other else core
        k = cidx(f, d, other)

        def put(at, t, v):
            Dd[k // 2, at, pl.ds(pl.multiple_of(cc * COLS + t * BS, BS), BS)] = v
        spread_d(Drow, k, put)

    def panel2(f, d):
        from_twin(f, d)
        panel(f, d, True)

    def chunk(b, f, e):
        return (1 - ylo if f else ylo) * 4 + (b + e) % 4

    dz = (z - x + 4) % 4
    o0 = (dz // 2) * (1 - dz % 2)
    o1 = 1 + 2 * (dz // 2)
    o2 = 4 - o0 - o1
    odd = (ylo + yhi) % 2
    plain = [chunk(x, 0, e) for e in range(4)] + [chunk(x, 1, e) for e in (o0, o1, o2 + 2 - (dz + 2) % 4, (dz + 2) % 4)]
    mixed = [chunk(z, 0, 0), chunk(x, 1, 0), chunk(z, 0, 1), chunk(z, 0, 3),
             chunk(x, 1, 1), chunk(x, 1, 3), chunk(x, 1, 2), chunk(z, 0, 2)]
    chunks = [(1 - odd) * a + odd * b for a, b in zip(plain, mixed)]

    def product(k):
        spread_d(Dcol, k, put_r)
        accS[...] += jnp.dot(Dd[k], Rd[...], preferred_element_type=F32)

    def products(n):
        def body(i, carry):
            product(chunks[n] + i * (chunks[n + 1] - chunks[n]))
            return carry
        lax.fori_loop(0, 2, body, 0)

    accS[...] = jnp.zeros_like(accS)
    accM[...] = jnp.zeros_like(accM)
    for c in later:
        c.wait()
    panel(0, 0, False)

    def relay(h):
        got(dc(1, 0, h), xr.at[h])
        push(Dcol.at[ridx(1, 0), h, pl.ds(0, SH)], zs.at[h], zr.at[h], yind, Drow.at[col, h])

    relay(0)
    got(dc(0, -1, 0), xr.at[2])
    X(dc(0, -1, 0), 10, xp)
    got(dc(0, 1, 1), xr.at[5])
    X(dc(0, 1, 1), 11, xm)
    got(dr(0, -1, 0), zr.at[2])
    Z(dr(0, -1, 0), 10, zp)
    got(dr(0, 1, 1), zr.at[5])
    Z(dr(0, 1, 1), 11, zm)
    panel2(0, 0)
    relay(1)
    X(dc(1, 0, 0), 6, xp)
    X(dc(1, 0, 1), 9, xm)
    X(dc(1, 0, 1), 7, xp)
    X(dc(1, 0, 0), 8, xm)
    h_own(0)
    h_own(1)
    h_own(2)
    got(dr(0, -1, 1), zr.at[3])
    to_twin(0, -1)
    got(dr(0, 1, 0), zr.at[4])
    to_twin(0, 1)
    panel(0, -1, False)
    panel(0, 1, False)
    got(dr(1, 0, 0), zr.at[0])
    Z(dr(1, 0, 0), 6, zp)
    Z(dr(1, 0, 0), 8, zm)
    panel2(0, -1)
    panel2(0, 1)
    got(dc(0, 2, 0), xr.at[10])
    X(dc(0, 2, 0), 12, ylod)
    got(dc(0, 2, 1), xr.at[11])
    X(dc(0, 2, 1), 13, ylod)
    got(dr(0, 2, 0), zr.at[10])
    got(dr(0, 2, 1), zr.at[11])
    to_twin(0, 2)
    got(dr(1, 0, 1), zr.at[1])
    Z(dr(1, 0, 1), 7, zp)
    Z(dr(1, 0, 1), 9, zm)
    to_twin(1, 0)
    panel(0, 2, False)
    panel(1, 0, False)
    panel2(0, 2)
    panel2(1, 0)
    got(dc(0, -1, 1), xr.at[3])
    got(dc(0, 1, 0), xr.at[4])
    products(0)
    got(dr(1, -1, 0), zr.at[6])
    Z(dr(1, -1, 0), 12, zp)
    got(dr(1, 1, 1), zr.at[9])
    Z(dr(1, 1, 1), 13, zm)
    got(dr(1, -1, 1), zr.at[7])
    to_twin(1, -1)
    got(dr(1, 1, 0), zr.at[8])
    to_twin(1, 1)
    panel(1, -1, False)
    panel(1, 1, False)
    panel2(1, -1)
    panel2(1, 1)
    got(dc(1, -1, 0), xr.at[6])
    got(dc(1, 1, 1), xr.at[9])
    got(dc(1, -1, 1), xr.at[7])
    got(dc(1, 1, 0), xr.at[8])
    products(2)
    h_mid(0)
    h_own(3)
    products(4)
    got(dc(1, 2, 0), xr.at[12])
    got(dc(1, 2, 1), xr.at[13])
    push(Dcol.at[:, 1 - core, pl.ds(SH, IND)], ts.at[NP + 1], tr.at[NP + 1], twin, Hti)
    got(dr(1, 2, 0), zr.at[12])
    got(dr(1, 2, 1), zr.at[13])
    to_twin(1, 2)
    h_mid(1)
    h_far(0)
    h_own(4)
    product(chunks[6])
    panel(1, 2, False)
    panel2(1, 2)
    product(chunks[7])

    Sown[...] = accS[...].astype(BF16)
    push(Sown, ts.at[NP], tr.at[NP], twin, Stw)
    h_mid(2)
    h_far(1)
    h_own(5)
    h_end(0)
    h_twin(0)
    out_s = pltpu.make_async_copy(Sown, s_out, loc.at[0])
    out_s.start()
    got(Hti, tr.at[NP + 1])

    def pick(acc, i, which):
        at = pl.ds(pl.multiple_of(i * BS, BS), BS)
        place = jnp.full((BS, BS), which, jnp.int32)
        out = acc[at, pl.ds(0, BS)]
        for t in range(1, CB):
            out = jnp.where(place == t, acc[at, pl.ds(t * BS, BS)], out)
        return out

    NT = (((1,), (1,)), ((), ()))

    def partials(q):
        def rows(m, carry):
            def put(ref):
                def store(ii, t, v):
                    at = pl.ds(pl.multiple_of(m * 64 + ii * JP, JP), JP)
                    ref[at, pl.ds(t * BS, BS)] = v
                return store
            own = Dcol[m, core, pl.ds(SH, IND), :].astype(F32)
            spread(lambda b: Hcol[q, m, core, b], own, put(Hr0))
            spread(lambda b: Htw[q, m, b], Hti[m].astype(F32), put(Hr1))
            return carry
        lax.fori_loop(0, 8, rows, 0)

        @pl.when(q == 0)
        def _():
            got(Stw, tr.at[NP])

        CT[q % 2] = (
            lax.dot_general(Hr0[...], Sown[...], NT, preferred_element_type=F32)
            + lax.dot_general(Hr1[...], Stw[...], NT, preferred_element_type=F32)
        )

    def extract(q, m, half, emit):
        ind = Drow[2 * m + core, half, pl.ds(HALF, IND), :].astype(F32)
        for ii in range(4):
            lanes = pl.ds((half * 4 + ii) * BS, BS)
            v = [CT[q % 2, pl.ds(pl.multiple_of(m * 64 + t * JP, JP), JP), lanes] for t in range(CB)]
            for s in range(KS):
                out = v[0]
                for t in range(1, CB):
                    k = ii * 8 + s * 4 + t
                    hit = jnp.broadcast_to(ind[k:k + 1], (JP, BS)) > 0.5
                    out = jnp.where(hit, v[t], out)
                emit(ii * KS + s, out)

    def chip(f, d):
        hh = (1 - yhi) if f else yhi
        return hh * 4 + (z + d + 4) % 4

    def rs_far(q):
        for f in (1, 0):
            m = chip(f, 2)
            for half, (dev, dst) in enumerate(((zp, Al), (zm, Ar))):
                def emit(b, v, half=half):
                    PB[q, m, half * 8 + b] = v.astype(BF16)
                extract(q, m, half, emit)
                i = q * 4 + f * 2 + half
                remote(PB.at[q, m, pl.ds(half * 8, 8)], dst.at[q, f], as_.at[i], ar.at[i], dev).start()

    def rs_near(q):
        for f in (1, 0):
            for side, (d, dev, src, dst) in enumerate(((1, zp, Al, Bl), (-1, zm, Ar, Br))):
                m = chip(f, d)
                i = q * 4 + f * 2 + side
                got(src.at[q, f], ar.at[i])
                for half in (0, 1):
                    def emit(b, v, half=half):
                        if half == side:
                            v = v + src[q, f, b].astype(F32)
                        PB[q, m, half * 8 + b] = v.astype(BF16)
                    extract(q, m, half, emit)
                remote(PB.at[q, m], dst.at[q, f], bs.at[i], br.at[i], dev).start()

    def rs_keep(q):
        for f in (1, 0):
            for half in (0, 1):
                def emit(b, v, half=half):
                    OWN[q % 3, f, half * 8 + b] = v
                extract(q, chip(f, 0), half, emit)

    def rs_own(q):
        for f in (1, 0):
            m = chip(f, 0)
            got(Bl.at[q, f], br.at[q * 4 + f * 2])
            got(Br.at[q, f], br.at[q * 4 + f * 2 + 1])
            for b in range(RB * KS):
                v = OWN[q % 3, f, b] + Bl[q, f, b].astype(F32) + Br[q, f, b].astype(F32)
                if f:
                    PB[q, m, b] = v.astype(BF16)
                else:
                    cub[b, pl.ds(pl.multiple_of(q * JP, JP), JP), :] = v
            if f:
                remote(PB.at[q, m], Y.at[q], ys.at[q], yr.at[q], yhid).start()

    def m_chunk(k):
        def body(half, c):
            ind = Dcol[k, half, pl.ds(SH, IND), :].astype(F32)

            def store(ii, t, v):
                Rd[pl.ds(pl.multiple_of(half * 512 + ii * BS, BS), BS), pl.ds(t * BS, BS)] = v

            spread(lambda b: Hcol[:, k, half, b].reshape(BS, BS), ind, store)
            return c
        lax.fori_loop(0, 2, body, 0)
        accM[...] += jnp.dot(Dd[k], Rd[...], preferred_element_type=F32)

    def m_order(n):
        m, late = n % 4, n // 4
        f = (1 - late) * (m * (3 - m) * (2 - m) // 2) + late * (1 - (m // 2) * (1 - m % 2))
        d = (1 - late) * ((m // 2) * (2 * m - 3)) + late * ((1 - m // 2) * (1 + 2 * m) + 2 * (m // 2))
        return ((ylo + f) % 2) * 4 + (x + d + 4) % 4

    def step(q, carry):
        @pl.when(q + 2 < NP)
        def _():
            h_far(q + 2)

        @pl.when(q + 3 < NP)
        def _():
            h_mid(q + 3)

        @pl.when(q + 6 < NP)
        def _():
            h_own(q + 6)

        @pl.when(q < NP)
        def _():
            got(Htw.at[q], tr.at[q])
            partials(q)
            rs_far(q)

        @pl.when((q >= 1) & (q < NP + 1))
        def _():
            rs_near(q - 1)
            rs_keep(q - 1)

        @pl.when(q >= 3)
        def _():
            rs_own(q - 3)

        @pl.when(q + 1 < NP)
        def _():
            h_end(q + 1)
            h_twin(q + 1)

        @pl.when(q >= NP - 4)
        def _():
            m_chunk(m_order(q - NP + 4))

        return carry

    lax.fori_loop(0, NP + 3, step, 0)
    m_chunk(m_order(7))

    Mout[...] = accM[...].astype(BF16)
    out_m = pltpu.make_async_copy(Mout, m_out, loc.at[1])
    out_m.start()

    def direct(i, carry):
        for s in range(KS):
            b = i * KS + s
            cub[b] = 3.0 * pick(accM, i, dcols[s, i] - col * CB) - 2.0 * cub[b].T
        return carry

    lax.fori_loop(0, RB, direct, 0)

    def y_wait(q, carry):
        got(Y.at[q], yr.at[q])
        return carry

    lax.fori_loop(0, NP, y_wait, 0)

    def gradient(b, carry):
        g_out[b] = (cub[b] - 2.0 * Y[:, b].reshape(BS, BS).astype(F32).T).astype(BF16)
        return carry

    lax.fori_loop(0, RB * KS, gradient, 0)
    out_s.wait()
    out_m.wait()

    for c in sends:
        c.wait_send()

    def drain(q, carry):
        for f, d, half, i, dev in H_OWN + H_MID + H_FAR:
            sent(hp(q, f, d, half), hs.at[q * HS + i])
        sent(Htw.at[q], ts.at[q])
        for i in range(4):
            sent(Al.at[q, 0], as_.at[q * 4 + i])
            sent(Bl.at[q, 0], bs.at[q * 4 + i])
        sent(Y.at[q], ys.at[q])
        return carry

    lax.fori_loop(0, NP, drain, 0)


def place_kernel(filt, s_in, m_in, g_in, s_out, m_out, g_out, sv, mv, gv, st, mt, came, went):
    ins = [pltpu.make_async_copy(a, v, came.at[n])
           for n, (a, v) in enumerate(((s_in, sv), (m_in, mv), (g_in, gv)))]
    for c in ins:
        c.start()
    outs = []
    for n, (v, to, out) in enumerate(((sv, st, s_out), (mv, mt, m_out))):
        ins[n].wait()
        for i in range(RB):
            for w in range(CB):
                lanes = pl.ds(pl.multiple_of(filt[w, i] % CB * BS, BS), BS)
                to[i * CB + w] = v[pl.ds(i * BS, BS), lanes]
        outs.append(pltpu.make_async_copy(to, out, went.at[n]))
        outs[n].start()
    ins[2].wait()
    outs.append(pltpu.make_async_copy(gv, g_out, went.at[2]))
    outs[2].start()
    for c in outs:
        c.wait()


def local(density, density_cols, hamilton, hamilton_cols, filter_cols):
    hbm = pl.BlockSpec(memory_space=pl.ANY)
    vmem = pl.BlockSpec(memory_space=pltpu.VMEM)
    smem = pl.BlockSpec(memory_space=pltpu.SMEM)
    dma = lambda n: pltpu.SemaphoreType.DMA((n,))
    s, m, g = pl.pallas_call(
        kernel,
        out_shape=(
            jax.ShapeDtypeStruct((ROWS, COLS), BF16),
            jax.ShapeDtypeStruct((ROWS, COLS), BF16),
            jax.ShapeDtypeStruct((RB * KS, BS, BS), BF16),
        ),
        in_specs=[hbm] * 2 + [smem] * 2,
        out_specs=(hbm, hbm, vmem),
        scratch_shapes=[
            pltpu.VMEM((NR, 2, SH + IND, BS), BF16),
            pltpu.VMEM((NP, NR, 2, 8, JP, BS), BF16),
            pltpu.VMEM((NC, 2, SH, BS), BF16),
            pltpu.VMEM((NP, NR, 8, JP, BS), BF16),
            pltpu.VMEM((NR, IND, BS), BF16),
            pltpu.VMEM((ROWS, COLS), BF16),
            pltpu.VMEM((ROWS, COLS), BF16),
            pltpu.VMEM((ROWS, COLS), BF16),
            pltpu.VMEM((NR, ROWS, CHUNK), BF16),
            pltpu.VMEM((CHUNK, COLS), BF16),
            pltpu.VMEM((NR * CB * JP, COLS), BF16),
            pltpu.VMEM((NR * CB * JP, COLS), BF16),
            pltpu.VMEM((ROWS, COLS), F32),
            pltpu.VMEM((ROWS, COLS), F32),
            pltpu.VMEM((2, NR * CB * JP, ROWS), F32),
            pltpu.VMEM((NP, NR, RB * KS, JP, BS), BF16),
            pltpu.VMEM((3, 2, RB * KS, JP, BS), F32),
            pltpu.VMEM((NP, 2, RB, JP, BS), BF16),
            pltpu.VMEM((NP, 2, RB, JP, BS), BF16),
            pltpu.VMEM((NP, 2, RB * KS, JP, BS), BF16),
            pltpu.VMEM((NP, 2, RB * KS, JP, BS), BF16),
            pltpu.VMEM((NP, RB * KS, JP, BS), BF16),
            pltpu.VMEM((RB * KS, BS, BS), F32),
            dma(2 + NP), dma(14), dma(14), dma(14), dma(14), dma(HS * NP), dma(HS * NP),
            dma(8), dma(8), dma(NP + 2), dma(NP + 2), dma(4 * NP), dma(4 * NP),
            dma(4 * NP), dma(4 * NP), dma(NP), dma(NP),
        ],
        compiler_params=pltpu.CompilerParams(
            collective_id=0, has_side_effects=True, vmem_limit_bytes=67_000_000),
    )(density.reshape(2, HALF, BS), hamilton.reshape(2, 8, NP, JP, BS), density_cols.T, hamilton_cols.T)
    slots = jax.ShapeDtypeStruct((RB * CB, BS, BS), BF16)
    s, m, g = pl.pallas_call(
        place_kernel,
        out_shape=(slots, slots, jax.ShapeDtypeStruct((RB * KS, BS, BS), BF16)),
        in_specs=[smem] + [hbm] * 3,
        out_specs=(hbm,) * 3,
        scratch_shapes=[
            pltpu.VMEM((ROWS, COLS), BF16),
            pltpu.VMEM((ROWS, COLS), BF16),
            pltpu.VMEM((RB * KS, BS, BS), BF16),
            pltpu.VMEM((RB * CB, BS, BS), BF16),
            pltpu.VMEM((RB * CB, BS, BS), BF16),
            dma(3), dma(3),
        ],
    )(filter_cols.T, s, m, g)
    return (s.reshape(RB, CB, BS, BS), m.reshape(RB, CB, BS, BS), g.reshape(RB, KS, BS, BS))


def solution(mesh):
    blocks, cols = P("row", "col", None, None), P("row", "col")
    return jax.shard_map(
        local, mesh=mesh, in_specs=(blocks, cols, blocks, cols, cols),
        out_specs=(blocks,) * 3, check_vma=False)
```

```python
import jax
import jax.numpy as jnp
from jax import lax
from jax.experimental import pallas as pl
from jax.experimental.pallas import tpu as pltpu
from jax.sharding import PartitionSpec as P

MESH = pl.DeviceIdType.MESH
BF16, F32 = jnp.bfloat16, jnp.float32
BS = 128
RB, CB = 8, 4
NR, NC = 8, 16
KS = 2
HALF = 4 * KS * BS
IND = 4 * KS * CB
SH = HALF + IND
NP = 8
JP = BS // NP
HS = 8
ROWS, COLS, CHUNK = RB * BS, CB * BS, RB * BS


def remote(src, dst, send, recv, dev):
    return pltpu.make_async_remote_copy(
        src_ref=src, dst_ref=dst, send_sem=send, recv_sem=recv,
        device_id=dev, device_id_type=MESH,
    )


def kernel(dv, hv, dcols, hcols, s_out, m_out, g_out,
           Dcol, Hcol, Drow, Htw, Hti, Sown, Stw, Mout, Dd, Rd, Hr0, Hr1, accS, accM, CT,
           PB, OWN, Al, Ar, Bl, Br, Y, cub,
           loc, xs, xr, zs, zr, hs, hr, cs, cr, ts, tr, as_, ar, bs, br, ys, yr):
    row, col = lax.axis_index("row"), lax.axis_index("col")
    x, ylo = row % 4, row // 4
    core, z, yhi = col % 2, (col // 2) % 4, col // 8

    def ridx(f, d):
        yy = (1 - ylo) if f else ylo
        return yy * 4 + (x + d + 4) % 4

    def cidx(f, d, other=False):
        yy = (1 - yhi) if f else yhi
        cc = (1 - core) if other else core
        return yy * 8 + ((z + d + 4) % 4) * 2 + cc

    xp, xm = (ridx(0, 1), col), (ridx(0, -1), col)
    zp, zm = (row, cidx(0, 1)), (row, cidx(0, -1))
    ylod = (ridx(1, 0), col)
    yind = (ridx(1, 0), cidx(1, 0))
    yhid = (row, cidx(1, 0))
    twin = (row, cidx(0, 0, True))

    first = [
        pltpu.make_async_copy(dv, Dcol.at[row, :, pl.ds(0, HALF), :], loc.at[0]),
        pltpu.make_async_copy(dv, Drow.at[col, :, pl.ds(0, HALF), :], loc.at[1]),
    ]
    later = [
        pltpu.make_async_copy(hv.at[:, :, q], Hcol.at[q, row], loc.at[2 + q])
        for q in range(NP)
    ]
    for c in first + later:
        c.start()
    barrier = pltpu.get_barrier_semaphore()
    for dev in (xp, xm, zp, zm, ylod, yind, yhid, twin):
        pl.semaphore_signal(barrier, inc=1, device_id=dev, device_id_type=MESH)

    line = lax.broadcasted_iota(jnp.int32, (IND, BS), 0)

    def indicators(cols, half):
        place = jnp.zeros((IND, BS), jnp.int32)
        for ii in range(4):
            for s in range(KS):
                c = jnp.full((IND, BS), cols[s, half * 4 + ii] - col * CB, jnp.int32)
                place = jnp.where(line // CB == ii * KS + s, c, place)
        return jnp.where(place == line % CB, 1.0, 0.0).astype(BF16)

    for half in (0, 1):
        ind = indicators(dcols, half)
        Dcol[row, half, pl.ds(HALF, IND), :] = ind
        Drow[col, half, pl.ds(HALF, IND), :] = ind
        Dcol[row, half, pl.ds(SH, IND), :] = indicators(hcols, half)
    for c in first:
        c.wait()
    pl.semaphore_wait(barrier, 8)

    sends = []

    def push(view, send, recv, dev, there=None):
        c = remote(view, view if there is None else there, send, recv, dev)
        c.start()
        sends.append(c)

    def got(view, recv):
        remote(view, view, recv, recv, twin).wait_recv()

    def sent(view, send):
        remote(view, view, send, send, twin).wait_send()

    def dc(f, d, half=None):
        k = ridx(f, d)
        return Dcol.at[k] if half is None else Dcol.at[k, half]

    def dr(f, d, half=None, other=False):
        k = cidx(f, d, other)
        return Drow.at[k] if half is None else Drow.at[k, half]

    def X(view, i, dev):
        push(view, xs.at[i], xr.at[i], dev)

    def Z(view, i, dev):
        push(view, zs.at[i], zr.at[i], dev)

    def to_twin(f, d):
        i = f * 4 + (d + 4) % 4
        push(dr(f, d), cs.at[i], cr.at[i], twin)

    def from_twin(f, d):
        got(dr(f, d, other=True), cr.at[f * 4 + (d + 4) % 4])

    X(dc(0, 0, 0), 0, ylod)
    X(dc(0, 0, 1), 1, ylod)
    X(dc(0, 0, 0), 2, xp)
    X(dc(0, 0, 1), 5, xm)
    Z(dr(0, 0, 0), 2, zp)
    Z(dr(0, 0, 1), 5, zm)
    X(dc(0, 0, 1), 3, xp)
    X(dc(0, 0, 0), 4, xm)
    Z(dr(0, 0, 1), 3, zp)
    Z(dr(0, 0, 0), 4, zm)
    to_twin(0, 0)

    def hp(q, f, d, half=None):
        k = ridx(f, d)
        return Hcol.at[q, k] if half is None else Hcol.at[q, k, half]

    H_OWN = ((0, 0, None, 0, ylod), (0, 0, None, 1, xp), (0, 0, None, 2, xm))
    H_MID = ((0, -1, 0, 5, xp), (0, 1, 1, 6, xm), (1, 0, None, 3, xp), (1, 0, None, 4, xm))
    H_FAR = ((0, 2, None, 7, ylod),)

    def h_push(q, f, d, half, i, dev):
        view = hp(q, f, d, half)
        remote(view, view, hs.at[q * HS + i], hr.at[q * HS + i], dev).start()

    def h_own(q):
        for a in H_OWN:
            h_push(q, *a)

    def h_mid(q):
        got(hp(q, 0, -1), hr.at[q * HS + 1])
        h_push(q, *H_MID[0])
        got(hp(q, 0, 1), hr.at[q * HS + 2])
        h_push(q, *H_MID[1])
        got(hp(q, 1, 0), hr.at[q * HS])
        h_push(q, *H_MID[2])
        h_push(q, *H_MID[3])

    def h_far(q):
        got(hp(q, 0, 2, 0), hr.at[q * HS + 5])
        got(hp(q, 0, 2, 1), hr.at[q * HS + 6])
        h_push(q, *H_FAR[0])

    def h_end(q):
        got(hp(q, 1, -1), hr.at[q * HS + 3])
        got(hp(q, 1, 1), hr.at[q * HS + 4])
        got(hp(q, 1, 2), hr.at[q * HS + 7])

    def h_twin(q):
        remote(Hcol.at[q, :, 1 - core], Htw.at[q], ts.at[q], tr.at[q], twin).start()

    def spread(block, ind, store):
        for ii in range(4):
            b0, b1 = block(ii * 2), block(ii * 2 + 1)
            n = b0.shape[0] // 16
            for t in range(CB):
                k = ii * 8 + t
                i0 = jnp.broadcast_to(ind[k:k + 1], (16, BS)).astype(BF16) > 0.5
                i1 = jnp.broadcast_to(ind[k + 4:k + 5], (16, BS)).astype(BF16)
                out = jnp.where(i0[None], b0.reshape(n, 16, BS), b1.reshape(n, 16, BS) * i1[None])
                store(ii, t, out.reshape(n * 16, BS))

    def spread_d(src, k, put):
        def body(half, carry):
            ind = src[k, half, pl.ds(HALF, IND), :].astype(F32)

            def store(ii, t, v):
                put(pl.ds(pl.multiple_of(half * 512 + ii * BS, BS), BS), t, v)

            spread(lambda b: src[k, half, pl.ds(b * BS, BS), :], ind, store)
            return carry
        lax.fori_loop(0, 2, body, 0)

    def put_r(at, t, v):
        Rd[at, pl.ds(t * BS, BS)] = v

    def panel(f, d, other):
        cc = (1 - core) if other else core
        k = cidx(f, d, other)

        def put(at, t, v):
            Dd[k // 2, at, pl.ds(pl.multiple_of(cc * COLS + t * BS, BS), BS)] = v
        spread_d(Drow, k, put)

    def panel2(f, d):
        from_twin(f, d)
        panel(f, d, True)

    def chunk(b, f, e):
        return (1 - ylo if f else ylo) * 4 + (b + e) % 4

    dz = (z - x + 4) % 4
    o0 = (dz // 2) * (1 - dz % 2)
    o1 = 1 + 2 * (dz // 2)
    o2 = 4 - o0 - o1
    odd = (ylo + yhi) % 2
    plain = [chunk(x, 0, e) for e in range(4)] + [chunk(x, 1, e) for e in (o0, o1, o2 + 2 - (dz + 2) % 4, (dz + 2) % 4)]
    mixed = [chunk(z, 0, 0), chunk(x, 1, 0), chunk(z, 0, 1), chunk(z, 0, 3),
             chunk(x, 1, 1), chunk(x, 1, 3), chunk(x, 1, 2), chunk(z, 0, 2)]
    chunks = [(1 - odd) * a + odd * b for a, b in zip(plain, mixed)]

    def product(k):
        spread_d(Dcol, k, put_r)
        accS[...] += jnp.dot(Dd[k], Rd[...], preferred_element_type=F32)

    def products(n):
        def body(i, carry):
            product(chunks[n] + i * (chunks[n + 1] - chunks[n]))
            return carry
        lax.fori_loop(0, 2, body, 0)

    accS[...] = jnp.zeros_like(accS)
    accM[...] = jnp.zeros_like(accM)
    for c in later:
        c.wait()
    panel(0, 0, False)

    def relay(h):
        got(dc(1, 0, h), xr.at[h])
        push(Dcol.at[ridx(1, 0), h, pl.ds(0, SH)], zs.at[h], zr.at[h], yind, Drow.at[col, h])

    relay(0)
    got(dc(0, -1, 0), xr.at[2])
    X(dc(0, -1, 0), 10, xp)
    got(dc(0, 1, 1), xr.at[5])
    X(dc(0, 1, 1), 11, xm)
    got(dr(0, -1, 0), zr.at[2])
    Z(dr(0, -1, 0), 10, zp)
    got(dr(0, 1, 1), zr.at[5])
    Z(dr(0, 1, 1), 11, zm)
    panel2(0, 0)
    relay(1)
    X(dc(1, 0, 0), 6, xp)
    X(dc(1, 0, 1), 9, xm)
    X(dc(1, 0, 1), 7, xp)
    X(dc(1, 0, 0), 8, xm)
    h_own(0)
    h_own(1)
    h_own(2)
    got(dr(0, -1, 1), zr.at[3])
    to_twin(0, -1)
    got(dr(0, 1, 0), zr.at[4])
    to_twin(0, 1)
    panel(0, -1, False)
    panel(0, 1, False)
    got(dr(1, 0, 0), zr.at[0])
    Z(dr(1, 0, 0), 6, zp)
    Z(dr(1, 0, 0), 8, zm)
    panel2(0, -1)
    panel2(0, 1)
    got(dc(0, 2, 0), xr.at[10])
    X(dc(0, 2, 0), 12, ylod)
    got(dc(0, 2, 1), xr.at[11])
    X(dc(0, 2, 1), 13, ylod)
    got(dr(0, 2, 0), zr.at[10])
    got(dr(0, 2, 1), zr.at[11])
    to_twin(0, 2)
    got(dr(1, 0, 1), zr.at[1])
    Z(dr(1, 0, 1), 7, zp)
    Z(dr(1, 0, 1), 9, zm)
    to_twin(1, 0)
    panel(0, 2, False)
    panel(1, 0, False)
    panel2(0, 2)
    panel2(1, 0)
    got(dc(0, -1, 1), xr.at[3])
    got(dc(0, 1, 0), xr.at[4])
    products(0)
    got(dr(1, -1, 0), zr.at[6])
    Z(dr(1, -1, 0), 12, zp)
    got(dr(1, 1, 1), zr.at[9])
    Z(dr(1, 1, 1), 13, zm)
    got(dr(1, -1, 1), zr.at[7])
    to_twin(1, -1)
    got(dr(1, 1, 0), zr.at[8])
    to_twin(1, 1)
    panel(1, -1, False)
    panel(1, 1, False)
    panel2(1, -1)
    panel2(1, 1)
    got(dc(1, -1, 0), xr.at[6])
    got(dc(1, 1, 1), xr.at[9])
    got(dc(1, -1, 1), xr.at[7])
    got(dc(1, 1, 0), xr.at[8])
    h_mid(0)
    h_own(3)
    products(2)
    h_mid(1)
    h_own(4)
    products(4)
    got(dc(1, 2, 0), xr.at[12])
    got(dc(1, 2, 1), xr.at[13])
    push(Dcol.at[:, 1 - core, pl.ds(SH, IND)], ts.at[NP + 1], tr.at[NP + 1], twin, Hti)
    got(dr(1, 2, 0), zr.at[12])
    got(dr(1, 2, 1), zr.at[13])
    to_twin(1, 2)
    h_mid(2)
    h_far(0)
    h_own(5)
    product(chunks[6])
    h_mid(3)
    h_far(1)
    h_own(6)
    panel(1, 2, False)
    panel2(1, 2)
    h_end(0)
    h_twin(0)
    product(chunks[7])

    Sown[...] = accS[...].astype(BF16)
    push(Sown, ts.at[NP], tr.at[NP], twin, Stw)
    h_mid(4)
    h_far(2)
    h_own(7)
    out_s = pltpu.make_async_copy(Sown, s_out, loc.at[0])
    out_s.start()
    got(Hti, tr.at[NP + 1])

    def pick(acc, i, which):
        at = pl.ds(pl.multiple_of(i * BS, BS), BS)
        place = jnp.full((BS, BS), which, jnp.int32)
        out = acc[at, pl.ds(0, BS)]
        for t in range(1, CB):
            out = jnp.where(place == t, acc[at, pl.ds(t * BS, BS)], out)
        return out

    NT = (((1,), (1,)), ((), ()))

    def partials(q):
        def rows(m, carry):
            def put(ref):
                def store(ii, t, v):
                    at = pl.ds(pl.multiple_of(m * (CB * JP) + ii * JP, JP), JP)
                    ref[at, pl.ds(t * BS, BS)] = v
                return store
            own = Dcol[m, core, pl.ds(SH, IND), :].astype(F32)
            spread(lambda b: Hcol[q, m, core, b], own, put(Hr0))
            spread(lambda b: Htw[q, m, b], Hti[m].astype(F32), put(Hr1))
            return carry
        lax.fori_loop(0, 8, rows, 0)

        @pl.when(q == 0)
        def _():
            got(Stw, tr.at[NP])

        CT[q % 2] = (
            lax.dot_general(Hr0[...], Sown[...], NT, preferred_element_type=F32)
            + lax.dot_general(Hr1[...], Stw[...], NT, preferred_element_type=F32)
        ).astype(BF16)

    def extract(q, m, half, emit):
        ind = Drow[2 * m + core, half, pl.ds(HALF, IND), :].astype(F32)
        for ii in range(4):
            lanes = pl.ds((half * 4 + ii) * BS, BS)
            v = [CT[q % 2, pl.ds(pl.multiple_of(m * (CB * JP) + t * JP, JP), JP), lanes] for t in range(CB)]
            for s in range(KS):
                out = v[0]
                for t in range(1, CB):
                    k = ii * 8 + s * 4 + t
                    hit = jnp.broadcast_to(ind[k:k + 1], (JP, BS)).astype(BF16) > 0.5
                    out = jnp.where(hit, v[t], out)
                emit(ii * KS + s, out)

    def chip(f, d):
        hh = (1 - yhi) if f else yhi
        return hh * 4 + (z + d + 4) % 4

    def rs_far(q):
        for f in (1, 0):
            m = chip(f, 2)
            for half, (dev, dst) in enumerate(((zp, Al), (zm, Ar))):
                def emit(b, v, half=half):
                    PB[q, m, half * 8 + b] = v.astype(BF16)
                extract(q, m, half, emit)
                i = q * 4 + f * 2 + half
                remote(PB.at[q, m, pl.ds(half * 8, 8)], dst.at[q, f], as_.at[i], ar.at[i], dev).start()

    def rs_near(q):
        for f in (1, 0):
            for side, (d, dev, src, dst) in enumerate(((1, zp, Al, Bl), (-1, zm, Ar, Br))):
                m = chip(f, d)
                i = q * 4 + f * 2 + side
                got(src.at[q, f], ar.at[i])
                for half in (0, 1):
                    def emit(b, v, half=half):
                        if half == side:
                            v = v.astype(F32) + src[q, f, b].astype(F32)
                        PB[q, m, half * 8 + b] = v.astype(BF16)
                    extract(q, m, half, emit)
                remote(PB.at[q, m], dst.at[q, f], bs.at[i], br.at[i], dev).start()

    def rs_keep(q):
        for f in (1, 0):
            for half in (0, 1):
                def emit(b, v, half=half):
                    OWN[q % 3, f, half * 8 + b] = v
                extract(q, chip(f, 0), half, emit)

    def rs_own(q):
        for f in (1, 0):
            m = chip(f, 0)
            got(Bl.at[q, f], br.at[q * 4 + f * 2])
            got(Br.at[q, f], br.at[q * 4 + f * 2 + 1])
            for b in range(RB * KS):
                v = OWN[q % 3, f, b].astype(F32) + Bl[q, f, b].astype(F32) + Br[q, f, b].astype(F32)
                if f:
                    PB[q, m, b] = v.astype(BF16)
                else:
                    cub[b, pl.ds(pl.multiple_of(q * JP, JP), JP), :] = v
            if f:
                remote(PB.at[q, m], Y.at[q], ys.at[q], yr.at[q], yhid).start()

    def m_chunk(k):
        def body(half, c):
            ind = Dcol[k, half, pl.ds(SH, IND), :].astype(F32)

            def store(ii, t, v):
                Rd[pl.ds(pl.multiple_of(half * 512 + ii * BS, BS), BS), pl.ds(t * BS, BS)] = v

            spread(lambda b: Hcol[:, k, half, b].reshape(BS, BS), ind, store)
            return c
        lax.fori_loop(0, 2, body, 0)
        accM[...] += jnp.dot(Dd[k], Rd[...], preferred_element_type=F32)

    def m_order(n):
        m, late = n % 4, n // 4
        f = (1 - late) * (m * (3 - m) * (2 - m) // 2) + late * (1 - (m // 2) * (1 - m % 2))
        d = (1 - late) * ((m // 2) * (2 * m - 3)) + late * ((1 - m // 2) * (1 + 2 * m) + 2 * (m // 2))
        return ((ylo + f) % 2) * 4 + (x + d + 4) % 4

    def step(q, carry):
        @pl.when(q + 5 < NP)
        def _():
            h_mid(q + 5)

        @pl.when(q + 3 < NP)
        def _():
            h_far(q + 3)

        @pl.when(q < NP)
        def _():
            got(Htw.at[q], tr.at[q])
            partials(q)
            rs_far(q)

        @pl.when((q >= 1) & (q < NP + 1))
        def _():
            rs_near(q - 1)
            rs_keep(q - 1)

        @pl.when(q >= 3)
        def _():
            rs_own(q - 3)

        @pl.when(q + 1 < NP)
        def _():
            h_end(q + 1)
            h_twin(q + 1)

        @pl.when(q >= NP - 5)
        def _():
            m_chunk(m_order(q - NP + 5))

        return carry

    lax.fori_loop(0, NP + 3, step, 0)

    Mout[...] = accM[...].astype(BF16)
    out_m = pltpu.make_async_copy(Mout, m_out, loc.at[1])
    out_m.start()

    def direct(i, carry):
        for s in range(KS):
            b = i * KS + s
            cub[b] = 3.0 * pick(accM, i, dcols[s, i] - col * CB) - 2.0 * cub[b].T
        return carry

    lax.fori_loop(0, RB, direct, 0)

    for c in sends:
        c.wait_send()

    def drain(q, carry):
        for f, d, half, i, dev in H_OWN + H_MID + H_FAR:
            sent(hp(q, f, d, half), hs.at[q * HS + i])
        sent(Htw.at[q], ts.at[q])
        for i in range(4):
            sent(Al.at[q, 0], as_.at[q * 4 + i])
            sent(Bl.at[q, 0], bs.at[q * 4 + i])
        sent(Y.at[q], ys.at[q])
        return carry

    lax.fori_loop(0, NP, drain, 0)

    def y_wait(q, carry):
        got(Y.at[q], yr.at[q])
        return carry

    lax.fori_loop(0, NP, y_wait, 0)

    def gradient(b, carry):
        g_out[b] = (cub[b] - 2.0 * Y[:, b].reshape(BS, BS).astype(F32).T).astype(BF16)
        return carry

    lax.fori_loop(0, RB * KS, gradient, 0)
    out_s.wait()
    out_m.wait()


def place_kernel(filt, s_in, m_in, g_in, s_out, m_out, g_out, sv, mv, gv, st, mt, came, went):
    ins = [pltpu.make_async_copy(a, v, came.at[n])
           for n, (a, v) in enumerate(((s_in, sv), (m_in, mv), (g_in, gv)))]
    for c in ins:
        c.start()
    outs = []
    for n, (v, to, out) in enumerate(((sv, st, s_out), (mv, mt, m_out))):
        ins[n].wait()
        for i in range(RB):
            for w in range(CB):
                lanes = pl.ds(pl.multiple_of(filt[w, i] % CB * BS, BS), BS)
                to[i * CB + w] = v[pl.ds(i * BS, BS), lanes]
        outs.append(pltpu.make_async_copy(to, out, went.at[n]))
        outs[n].start()
    ins[2].wait()
    outs.append(pltpu.make_async_copy(gv, g_out, went.at[2]))
    outs[2].start()
    for c in outs:
        c.wait()


def local(density, density_cols, hamilton, hamilton_cols, filter_cols):
    hbm = pl.BlockSpec(memory_space=pl.ANY)
    vmem = pl.BlockSpec(memory_space=pltpu.VMEM)
    smem = pl.BlockSpec(memory_space=pltpu.SMEM)
    dma = lambda n: pltpu.SemaphoreType.DMA((n,))
    s, m, g = pl.pallas_call(
        kernel,
        out_shape=(
            jax.ShapeDtypeStruct((ROWS, COLS), BF16),
            jax.ShapeDtypeStruct((ROWS, COLS), BF16),
            jax.ShapeDtypeStruct((RB * KS, BS, BS), BF16),
        ),
        in_specs=[hbm] * 2 + [smem] * 2,
        out_specs=(hbm, hbm, vmem),
        scratch_shapes=[
            pltpu.VMEM((NR, 2, SH + IND, BS), BF16),
            pltpu.VMEM((NP, NR, 2, 8, JP, BS), BF16),
            pltpu.VMEM((NC, 2, SH, BS), BF16),
            pltpu.VMEM((NP, NR, 8, JP, BS), BF16),
            pltpu.VMEM((NR, IND, BS), BF16),
            pltpu.VMEM((ROWS, COLS), BF16),
            pltpu.VMEM((ROWS, COLS), BF16),
            pltpu.VMEM((ROWS, COLS), BF16),
            pltpu.VMEM((NR, ROWS, CHUNK), BF16),
            pltpu.VMEM((CHUNK, COLS), BF16),
            pltpu.VMEM((NR * CB * JP, COLS), BF16),
            pltpu.VMEM((NR * CB * JP, COLS), BF16),
            pltpu.VMEM((ROWS, COLS), F32),
            pltpu.VMEM((ROWS, COLS), F32),
            pltpu.VMEM((2, NR * CB * JP, ROWS), BF16),
            pltpu.VMEM((NP, NR, RB * KS, JP, BS), BF16),
            pltpu.VMEM((3, 2, RB * KS, JP, BS), BF16),
            pltpu.VMEM((NP, 2, RB, JP, BS), BF16),
            pltpu.VMEM((NP, 2, RB, JP, BS), BF16),
            pltpu.VMEM((NP, 2, RB * KS, JP, BS), BF16),
            pltpu.VMEM((NP, 2, RB * KS, JP, BS), BF16),
            pltpu.VMEM((NP, RB * KS, JP, BS), BF16),
            pltpu.VMEM((RB * KS, BS, BS), F32),
            dma(2 + NP), dma(14), dma(14), dma(14), dma(14), dma(HS * NP), dma(HS * NP),
            dma(8), dma(8), dma(NP + 2), dma(NP + 2), dma(4 * NP), dma(4 * NP),
            dma(4 * NP), dma(4 * NP), dma(NP), dma(NP),
        ],
        compiler_params=pltpu.CompilerParams(
            collective_id=0, has_side_effects=True, vmem_limit_bytes=67_000_000),
    )(density.reshape(2, HALF, BS), hamilton.reshape(2, 8, NP, JP, BS), density_cols.T, hamilton_cols.T)
    slots = jax.ShapeDtypeStruct((RB * CB, BS, BS), BF16)
    s, m, g = pl.pallas_call(
        place_kernel,
        out_shape=(slots, slots, jax.ShapeDtypeStruct((RB * KS, BS, BS), BF16)),
        in_specs=[smem] + [hbm] * 3,
        out_specs=(hbm,) * 3,
        scratch_shapes=[
            pltpu.VMEM((ROWS, COLS), BF16),
            pltpu.VMEM((ROWS, COLS), BF16),
            pltpu.VMEM((RB * KS, BS, BS), BF16),
            pltpu.VMEM((RB * CB, BS, BS), BF16),
            pltpu.VMEM((RB * CB, BS, BS), BF16),
            dma(3), dma(3),
        ],
    )(filter_cols.T, s, m, g)
    return (s.reshape(RB, CB, BS, BS), m.reshape(RB, CB, BS, BS), g.reshape(RB, KS, BS, BS))


def solution(mesh):
    blocks, cols = P("row", "col", None, None), P("row", "col")
    return jax.shard_map(
        local, mesh=mesh, in_specs=(blocks, cols, blocks, cols, cols),
        out_specs=(blocks,) * 3, check_vma=False)
```
